512 devices in a mesh: dp: 32 (over x, y), ctx: 16 (over z, core).
Axes of the slice: x: 4, y: 8, z: 8, core: 2. Of those that a mesh axis runs over, the one named last changes fastest.
Arguments:
- keys_a: bfloat16 [32, 2048, 2560], P('dp', 'ctx'), may hold values from -6 to 6
- values_a: bfloat16 [32, 2048, 2560], P('dp', 'ctx'), may hold values from -6 to 6
- queries_b: bfloat16 [32, 2048, 2560], P('dp', 'ctx'), may hold values from -6 to 6
- grad_out: bfloat16 [32, 2048, 2560], P('dp', 'ctx'), may hold values from -1.5 to 1.5
- state_start: float32 [3, 20, 128, 128], P(None, None, 'ctx'), may hold values from -0.5 to 0.5
- state_next: float32 [32, 3, 20, 128, 128], P('dp', None, None, 'ctx'), may hold values from -0.5 to 0.5
Outputs:
- grad_keys: bfloat16 [32, 2048, 2560], P('dp', 'ctx')
- grad_values: bfloat16 [32, 2048, 2560], P('dp', 'ctx')
- grad_state: float32 [3, 20, 128, 128], P(None, None, 'ctx')
The draws below stay inside these ranges and needn't reach their ends.
All inputs are finite; a program needn't handle non-finite values.
Results may differ from the reference program's by a relative error of at most 0.033.
Values may be sent and summed in bfloat16 or wider, within the bound.
A program may use at most 128 MiB of HBM per device.

```python
import jax
import jax.numpy as jnp
from jax import lax

D = 128
H = 20
F = 128
NS_STEPS = 2
TOK = 128
CLIPS = 32
GROUP = 2048
N_DP = 32
N_CTX = 16


def steps_of(rng, dims, pieces, low, top_value):
    def one(axis_at, parts):
        heights = jax.random.uniform(jax.random.fold_in(jax.random.fold_in(rng, 6), axis_at), (parts,), jnp.float32, low / len(pieces), top_value / len(pieces))
        return jnp.repeat(jnp.exp(heights), dims[axis_at] // parts).reshape((-1,) + (1,) * (len(dims) - axis_at - 1))

    factor_of = one(*pieces[0])
    for cut in pieces[1:]:
        factor_of = factor_of * one(*cut)
    return factor_of


def bell_draw(rng, extent, width, limit, shards=(), held_as=jnp.bfloat16):
    drawn = width * jax.random.normal(rng, extent, jnp.float32)
    if shards:
        drawn = drawn * steps_of(rng, extent, shards, -0.22, 0.18)
    return jnp.clip(drawn, -limit, limit).astype(held_as)


def setup_inputs(seed: int = 0) -> dict:
    key_list = jax.random.split(jax.random.key(seed), 7)
    keys_a = bell_draw(key_list[0], (CLIPS, GROUP, H * D), 1.0, 6.0, ((0, 32), (1, 16)))
    values_a = bell_draw(key_list[1], (CLIPS, GROUP, H * D), 1.0, 6.0, ((0, 32), (1, 16)))
    queries_b = bell_draw(key_list[2], (CLIPS, GROUP, H * D), 1.0, 6.0, ((0, 32), (1, 16)))
    grad_out = bell_draw(key_list[3], (CLIPS, GROUP, H * D), 0.25, 1.5, ((0, 32), (1, 16)))
    state_start = bell_draw(key_list[4], (3, H, D, F), D ** -0.5, 0.5, ((2, 16),), jnp.float32)
    state_next = bell_draw(key_list[5], (CLIPS, 3, H, D, F), D ** -0.5, 0.5, ((0, 32), (3, 16)), jnp.float32)
    return {"keys_a": keys_a, "values_a": values_a, "queries_b": queries_b, "grad_out": grad_out, "state_start": state_start, "state_next": state_next}


step_rate = 4.0
coef_a = 3.4445
coef_b = -4.775
coef_c = 2.0315

def round_trip(value):
    return lax.optimization_barrier(value.astype(jnp.bfloat16)).astype(jnp.float32)

def field_grad(weights_in, inputs, targets):
    rounded = round_trip(weights_in)
    left_rows = inputs.astype(jnp.float32)
    right_rows = targets.astype(jnp.float32)
    gate_pre = jnp.einsum('thd,hdf->thf', left_rows, rounded[0])
    up_pre = jnp.einsum('thd,hdf->thf', left_rows, rounded[1])
    target_proj = jnp.einsum('thd,hdf->thf', right_rows, rounded[2])
    sigmoid_val = jax.nn.sigmoid(gate_pre)
    swish_val = gate_pre * sigmoid_val
    hidden = round_trip(swish_val * up_pre)
    d_gate = round_trip(target_proj * up_pre * sigmoid_val * (1.0 + gate_pre * (1.0 - sigmoid_val)))
    d_up = round_trip(target_proj * swish_val)
    grad_a = jnp.einsum('thd,thf->hdf', left_rows, d_gate)
    grad_b = jnp.einsum('thd,thf->hdf', left_rows, d_up)
    grad_c = jnp.einsum('thd,thf->hdf', right_rows, hidden)
    return jnp.stack([grad_a, grad_b, grad_c])

def newton(gradients):
    scale_norm = jnp.sqrt(lax.optimization_barrier(jnp.sum(gradients * gradients, axis=(1, 2), keepdims=True)) + 1e-06)
    iterate = round_trip(gradients / scale_norm)
    for repeat in range(NS_STEPS):
        gram_block = round_trip(jnp.einsum('mdf,mef->mde', iterate, iterate))
        square = jnp.einsum('mde,mek->mdk', gram_block, gram_block)
        poly_term = round_trip(coef_b * gram_block + coef_c * square)
        iterate = round_trip(coef_a * iterate + jnp.einsum('mde,mef->mdf', poly_term, iterate))
    return iterate

def reference(keys_a, values_a, queries_b, grad_out, state_start, state_next):
    block_shape = (N_CTX, TOK, H, D)
    slot_shape = (3 * H, D, F)

    def one_clip(blocks):
        key_blocks = blocks[0].reshape(block_shape)
        value_blocks = blocks[1].reshape(block_shape)
        query_blocks = blocks[2].reshape(block_shape)
        out_blocks = blocks[3].reshape(block_shape)
        clip_next = blocks[4]
        parts_g = jax.vmap(field_grad, in_axes=(None, 0, 0))(state_start, key_blocks, value_blocks)
        total_g = lax.optimization_barrier(jnp.sum(round_trip(parts_g), axis=0))
        parts_s = jax.vmap(field_grad, in_axes=(None, 0, 0))(clip_next, query_blocks, out_blocks)
        total_s = lax.optimization_barrier(jnp.sum(round_trip(parts_s), axis=0))
        d_update = round_trip(step_rate * total_s).reshape(slot_shape)
        unused, pullback = jax.vjp(newton, total_g.reshape(slot_shape))
        d_field = pullback(d_update)[0].reshape(total_g.shape)

        def backward(key_block, value_block):
            unused_out, pull_field = jax.vjp(field_grad, state_start, key_block, value_block)
            return pull_field(d_field)
        d_start, d_keys, d_values = jax.vmap(backward)(key_blocks, value_blocks)
        clip_state = lax.optimization_barrier(jnp.sum(round_trip(parts_s + d_start), axis=0))
        return (d_keys.reshape(GROUP, H * D).astype(jnp.bfloat16), d_values.reshape(GROUP, H * D).astype(jnp.bfloat16), clip_state)
    grad_keys, grad_values, clip_states = lax.map(one_clip, (keys_a, values_a, queries_b, grad_out, state_next))
    grad_state = lax.optimization_barrier(jnp.sum(clip_states, axis=0)) / N_DP
    return (grad_keys, grad_values, grad_state)
```

```python
import functools

import jax
import jax.numpy as jnp
from jax import lax
from jax.experimental import pallas as pl
from jax.experimental.pallas import tpu as pltpu
from jax.sharding import PartitionSpec as P

D = 128
H = 20
F = 128
HH = H // 2
RATE = 4.0
CA = 3.4445
CB = -4.775
CC = 2.0315
MESH = pl.DeviceIdType.MESH
F32 = jnp.float32
BF16 = jnp.bfloat16


def mm(a, b):
    return jnp.dot(a, b, preferred_element_type=F32)


def mm_tn(a, b):
    return lax.dot_general(a, b, (((0,), (0,)), ((), ())), preferred_element_type=F32)


def mm_nt(a, b):
    return lax.dot_general(a, b, (((1,), (1,)), ((), ())), preferred_element_type=F32)


def newton_forward(mats):
    norms, units, xs, grams, polys = [], [], [], [], []
    for g in mats:
        total = jnp.sum(jnp.sum(g * g, axis=1, keepdims=True), axis=0, keepdims=True)
        n = jnp.sqrt(total + 1e-06)
        u = g / n
        norms.append(n)
        units.append(u)
    x = [u.astype(BF16) for u in units]
    for step in range(2):
        a = [mm_nt(v, v).astype(BF16) for v in x]
        sq = [mm(v, v) for v in a]
        p = [(CB * v.astype(F32) + CC * w).astype(BF16) for v, w in zip(a, sq)]
        xs.append(x)
        grams.append(a)
        polys.append(p)
        if step == 0:
            mixed = [mm(v, w) for v, w in zip(p, x)]
            x = [(CA * v.astype(F32) + w).astype(BF16) for v, w in zip(x, mixed)]
    return norms, units, xs, grams, polys


def newton_backward(saved, cts):
    norms, units, xs, grams, polys = saved
    ct = cts
    for step in (1, 0):
        x, a, p = xs[step], grams[step], polys[step]
        ct_z = [mm_nt(v, w).astype(BF16) for v, w in zip(ct, x)]
        direct = [CA * v.astype(F32) + mm(w, v) for v, w in zip(ct, p)]
        ct_a = [
            (CB * v.astype(F32) + CC * (mm(v, w) + mm(w, v))).astype(BF16)
            for v, w in zip(ct_z, a)
        ]
        ct = [
            (d + mm(v, w) + mm_tn(v, w)).astype(BF16) for d, v, w in zip(direct, ct_a, x)
        ]
    out = []
    for n, u, v in zip(norms, units, ct):
        v = v.astype(F32)
        dot = jnp.sum(jnp.sum(v * u, axis=1, keepdims=True), axis=0, keepdims=True)
        out.append((v - u * dot) / n)
    return out


def main_kernel(
    nz,
    keys, values, queries, gout, start, nxt,
    dk_out, dv_out, part_out,
    xk, xv, xq, xo, stage, ws, wn, gbuf, sbuf, psum,
    rs_send, rs_recv, field, act, rnd, dk, dv, tot, gr_send, gr_recv,
    in_sem, x_ssem, x_rsem, ag_ssem, ag_rsem, rs_ssem, rs_rsem,
    f_ssem, f_rsem, gr_ssem, gr_rsem, o_sem, o_ssem, o_rsem,
):
    ctx = lax.axis_index("ctx")
    z = lax.div(ctx, 2)
    c = lax.rem(ctx, 2)
    other = 1 - c

    def chip(offset):
        return lax.rem(z + offset + 2 * nz, nz)

    right = 2 * chip(1) + c
    left = 2 * chip(-1) + c
    partner = 2 * z + other
    half = HH * D
    dirs = ((right, 1), (left, -1))
    far = nz // 2

    barrier = pltpu.get_barrier_semaphore()
    for peer in (right, left, partner):
        pl.semaphore_signal(barrier, inc=1, device_id={"ctx": peer}, device_id_type=MESH)
    pl.semaphore_wait(barrier, 3)

    def remote(src, dst, ssem, rsem, peer):
        return pltpu.make_async_remote_copy(
            src_ref=src, dst_ref=dst, send_sem=ssem, recv_sem=rsem,
            device_id={"ctx": peer}, device_id_type=MESH,
        )

    own_heads = pl.ds(c * HH, HH)
    other_heads = pl.ds(other * HH, HH)
    own_cols = pl.ds(pl.multiple_of(c * half, 128), half)
    other_cols = pl.ds(pl.multiple_of(other * half, 128), half)
    tokens = keys.shape[0]

    sends = []
    locals_in, remotes_in = [], []
    for k, st in enumerate((start, nxt)):
        cp = remote(st.at[:, other_heads], stage.at[k, c], x_ssem.at[k], x_rsem.at[k], partner)
        cp.start()
        remotes_in.append(cp)
        lc = pltpu.make_async_copy(st.at[:, own_heads], stage.at[k, 2], in_sem.at[k])
        lc.start()
        locals_in.append(lc)
    for k, (src, dst) in enumerate(((keys, xk), (values, xv), (queries, xq), (gout, xo))):
        cp = remote(
            src.at[:, other_cols], dst.at[tokens : 2 * tokens],
            x_ssem.at[2 + k], x_rsem.at[2 + k], partner,
        )
        cp.start()
        remotes_in.append(cp)
        lc = pltpu.make_async_copy(src.at[:, own_cols], dst.at[0:tokens], in_sem.at[2 + k])
        lc.start()
        locals_in.append(lc)
    sends.extend(remotes_in)

    def rows_of(offset):
        return pl.ds(pl.multiple_of(16 * chip(offset), 16), 16)

    weights = (ws, wn)
    for k in range(2):
        locals_in[k].wait()
        remotes_in[k].wait_recv()
        mine = stage[k, 2]
        theirs = stage[k, other]
        for comp in range(3):
            top = jnp.where(c == 0, mine[comp], theirs[comp])
            low = jnp.where(c == 0, theirs[comp], mine[comp])
            weights[k][:, rows_of(0), comp * F : (comp + 1) * F] = jnp.concatenate(
                [top, low], axis=1
            ).astype(BF16)

    def ag_copy(k, dr, step):
        peer, sign = dirs[dr]
        heads = pl.ds(0, HH)
        if step == far:
            heads = pl.ds(0, HH // 2) if dr == 0 else pl.ds(HH // 2, HH - HH // 2)
        piece = weights[k].at[heads, rows_of(-sign * (step - 1)), :]
        return remote(piece, piece, ag_ssem.at[k, dr, step - 1], ag_rsem.at[k, dr, step - 1], peer)

    ag = {}
    for step in range(1, far + 1):
        for k in range(2):
            for dr in range(2):
                if step > 1:
                    ag[k, dr, step - 1].wait_recv()
                cp = ag_copy(k, dr, step)
                cp.start()
                ag[k, dr, step] = cp
                sends.append(cp)
    for k in range(4):
        locals_in[2 + k].wait()
        remotes_in[2 + k].wait_recv()

    def phi(h, xs, ys, w):
        cols = pl.ds(pl.multiple_of(h * D, 128), D)
        x, y = xs[:, cols], ys[:, cols]
        wh = w[h]
        gu = mm(x, wh[:, : 2 * F])
        proj = mm(y, wh[:, 2 * F :])
        gate, up = gu[:, :F], gu[:, F:]
        s = jax.nn.sigmoid(gate)
        swish = gate * s
        hidden = (swish * up).astype(BF16)
        d_gate = (proj * up * s * (1.0 + gate * (1.0 - s))).astype(BF16)
        d_up = (proj * swish).astype(BF16)
        gab = mm_tn(x, jnp.concatenate([d_gate, d_up], axis=1))
        gc = mm_tn(y, hidden)
        return gate, up, proj, hidden, d_gate, d_up, gab, gc

    def phi_a(h, carry):
        gate, up, proj, hidden, d_gate, d_up, gab, gc = phi(h, xk, xv, ws)
        act[h, 0] = gate
        act[h, 1] = up
        act[h, 2] = proj
        rnd[h, 0] = d_gate
        rnd[h, 1] = d_up
        rnd[h, 2] = hidden
        gbuf[3 * h] = gab[:, :F].astype(BF16)
        gbuf[3 * h + 1] = gab[:, F:].astype(BF16)
        gbuf[3 * h + 2] = gc.astype(BF16)
        return carry

    def phi_b(h, carry):
        _, _, _, _, _, _, gab, gc = phi(h, xq, xo, wn)
        psum[h, :, : 2 * F] = gab
        psum[h, :, 2 * F :] = gc
        sbuf[3 * h] = gab[:, :F].astype(BF16)
        sbuf[3 * h + 1] = gab[:, F:].astype(BF16)
        sbuf[3 * h + 2] = gc.astype(BF16)
        return carry

    for pad in (3 * HH, 3 * HH + 1):
        gbuf[pad] = jnp.zeros((D, F), BF16)
        sbuf[pad] = jnp.zeros((D, F), BF16)

    bufs = (gbuf, sbuf)
    rs = {}

    def rs_step(k, step):
        for dr, (peer, sign) in enumerate(dirs):
            base = pl.multiple_of(4 * chip(sign * (far + 1 - step)), 4)
            lo, cnt = (0, 4)
            if step == 1:
                lo, cnt = (0, 2) if dr == 0 else (2, 2)
            value = bufs[k][pl.ds(base + lo, cnt)]
            if step > 1:
                rs[k, dr, step - 1].wait_recv()
                if step == 2:
                    plo = 0 if dr == 0 else 2
                    for j in range(4):
                        v = bufs[k][base + j]
                        if plo <= j < plo + 2:
                            v = (v.astype(F32) + rs_recv[k, dr, 0, j].astype(F32)).astype(BF16)
                        rs_send[k, dr, 1, j] = v
                else:
                    total = value.astype(F32) + rs_recv[k, dr, step - 2].astype(F32)
                    rs_send[k, dr, step - 1] = total.astype(BF16)
                src = rs_send.at[k, dr, step - 1]
            else:
                src = bufs[k].at[pl.ds(base + lo, cnt)]
            dst = rs_recv.at[k, dr, step - 1, pl.ds(lo, cnt)]
            cp = remote(src, dst, rs_ssem.at[k, dr, step - 1], rs_rsem.at[k, dr, step - 1], peer)
            cp.start()
            rs[k, dr, step] = cp
            sends.append(cp)

    def rs_total(k):
        out = []
        for dr in range(2):
            rs[k, dr, far].wait_recv()
        base = pl.multiple_of(4 * z, 4)
        for j in range(4):
            v = bufs[k][base + j].astype(F32)
            v = v + rs_recv[k, 0, far - 1, j].astype(F32) + rs_recv[k, 1, far - 1, j].astype(F32)
            out.append(v)
        return out

    ag[0, 0, far].wait_recv()
    ag[0, 1, far].wait_recv()
    lax.fori_loop(0, HH, phi_a, 0)
    rs_step(0, 1)
    ag[1, 0, far].wait_recv()
    ag[1, 1, far].wait_recv()
    cuts = [HH * i // far for i in range(far + 1)]
    for i in range(far):
        lax.fori_loop(cuts[i], cuts[i + 1], phi_b, 0)
        if i + 2 <= far:
            rs_step(0, i + 2)
    rs_step(1, 1)
    saved = newton_forward(rs_total(0))
    for step in range(2, far + 1):
        rs_step(1, step)
    cts = [(RATE * v).astype(BF16) for v in rs_total(1)]
    fields = newton_backward(saved, cts)
    for j in range(4):
        field[pl.multiple_of(4 * z, 4) + j] = fields[j].astype(BF16)

    fd = {}
    for step in range(1, far + 1):
        for dr, (peer, sign) in enumerate(dirs):
            if step > 1:
                fd[dr, step - 1].wait_recv()
            base = pl.multiple_of(4 * chip(-sign * (step - 1)), 4)
            lo, cnt = (0, 4)
            if step == far:
                lo, cnt = (0, 2) if dr == 0 else (2, 2)
            piece = field.at[pl.ds(base + lo, cnt)]
            cp = remote(piece, piece, f_ssem.at[dr, step - 1], f_rsem.at[dr, step - 1], peer)
            cp.start()
            fd[dr, step] = cp
            sends.append(cp)
    fd[0, far].wait_recv()
    fd[1, far].wait_recv()

    def back(h, carry):
        cols = pl.ds(pl.multiple_of(h * D, 128), D)
        x, y = xk[:, cols], xv[:, cols]
        gate, up, proj = act[h, 0], act[h, 1], act[h, 2]
        d_gate, d_up, hidden = rnd[h, 0], rnd[h, 1], rnd[h, 2]
        da, db, dc = field[3 * h], field[3 * h + 1], field[3 * h + 2]
        dab = jnp.concatenate([da, db], axis=1)
        ct_gu = mm(x, dab).astype(BF16).astype(F32)
        ct_dg, ct_du = ct_gu[:, :F], ct_gu[:, F:]
        ct_h = mm(y, dc).astype(BF16).astype(F32)
        s = jax.nn.sigmoid(gate)
        swish = gate * s
        sd = s * (1.0 - s)
        q = s + gate * sd
        qd = sd * (2.0 + gate * (1.0 - 2.0 * s))
        ct_w = ct_h * up + ct_du * proj
        cq = ct_dg * q
        ct_up = (ct_h * swish + cq * proj).astype(BF16)
        ct_p = (ct_du * swish + cq * up).astype(BF16)
        ct_gate = (ct_w * q + ct_dg * (proj * up) * qd).astype(BF16)
        wh = ws[h]
        ct_ab = jnp.concatenate([ct_gate, ct_up], axis=1)
        d_ab = jnp.concatenate([d_gate, d_up], axis=1)
        dx = mm_nt(d_ab, dab) + mm_nt(ct_ab, wh[:, : 2 * F])
        dy = mm_nt(hidden, dc) + mm_nt(ct_p, wh[:, 2 * F :])
        dk[:, cols] = dx.astype(BF16)
        dv[:, cols] = dy.astype(BF16)
        tot[h, :, : 2 * F] = (psum[h, :, : 2 * F] + mm_tn(x, ct_ab)).astype(BF16)
        tot[h, :, 2 * F :] = (psum[h, :, 2 * F :] + mm_tn(y, ct_p)).astype(BF16)
        return carry

    lax.fori_loop(0, HH, back, 0)

    outs = []
    for k, (src, dst) in enumerate(((dk, dk_out), (dv, dv_out))):
        cp = remote(src.at[tokens : 2 * tokens], dst.at[:, own_cols], o_ssem.at[k], o_rsem.at[k], partner)
        lc = pltpu.make_async_copy(src.at[0:tokens], dst.at[:, own_cols], o_sem.at[k])
        outs.append((cp, lc))

    gr = {}
    for step in range(1, far + 1):
        for dr, (peer, sign) in enumerate(dirs):
            rows = rows_of(sign * (far + 1 - step))
            lo, cnt = 0, HH
            if step == 1:
                lo, cnt = (0, HH // 2) if dr == 0 else (HH // 2, HH - HH // 2)
                src = tot.at[pl.ds(lo, cnt), rows, :]
            else:
                gr[dr, step - 1].wait_recv()
                if step == 2:
                    a, b = (0, HH // 2) if dr == 0 else (HH // 2, HH)
                    own = tot[a:b, rows, :].astype(F32) + gr_recv[dr, 0, a:b].astype(F32)
                    gr_send[dr, 1, a:b] = own.astype(BF16)
                    a, b = (HH // 2, HH) if dr == 0 else (0, HH // 2)
                    gr_send[dr, 1, a:b] = tot[a:b, rows, :]
                else:
                    own = tot[:, rows, :].astype(F32) + gr_recv[dr, step - 2].astype(F32)
                    gr_send[dr, step - 1] = own.astype(BF16)
                src = gr_send.at[dr, step - 1]
            dst = gr_recv.at[dr, step - 1, pl.ds(lo, cnt)]
            cp = remote(src, dst, gr_ssem.at[dr, step - 1], gr_rsem.at[dr, step - 1], peer)
            cp.start()
            gr[dr, step] = cp
            sends.append(cp)
        if step == 1:
            for cp, lc in outs:
                cp.start()
                lc.start()
    gr[0, far].wait_recv()
    gr[1, far].wait_recv()
    own = tot[:, rows_of(0), :].astype(F32)
    own = own + gr_recv[0, far - 1].astype(F32) + gr_recv[1, far - 1].astype(F32)
    own = own.astype(BF16)
    for h in range(HH):
        for comp in range(3):
            part_out[3 * h + comp] = own[h, :, comp * F : (comp + 1) * F]
    part_out[3 * HH] = jnp.zeros((16, F), BF16)
    part_out[3 * HH + 1] = jnp.zeros((16, F), BF16)

    for cp in sends:
        cp.wait_send()
    for cp, lc in outs:
        cp.wait_send()
        cp.wait_recv()
        lc.wait()


def dp_kernel(n, part, out, land, fin, stage, s1, r1, s2, r2, o_sem, o_ssem, o_rsem):
    ctx = lax.axis_index("ctx")
    c = lax.rem(ctx, 2)
    other = 1 - c
    partner = ctx + 1 - 2 * c
    me = lax.axis_index("dp")
    barrier = pltpu.get_barrier_semaphore()

    def peer_of(k):
        return lax.rem(me + k, n)

    def greet(k, carry):
        pl.semaphore_signal(barrier, inc=1, device_id={"dp": peer_of(k)}, device_id_type=MESH)
        return carry

    lax.fori_loop(1, n, greet, 0)
    pl.semaphore_signal(barrier, inc=1, device_id={"ctx": partner}, device_id_type=MESH)
    pl.semaphore_wait(barrier, n)

    def scatter(k):
        j = peer_of(k)
        return pltpu.make_async_remote_copy(
            src_ref=part.at[j], dst_ref=land.at[k], send_sem=s1.at[k], recv_sem=r1.at[k],
            device_id={"dp": j}, device_id_type=MESH,
        )

    def spread(k):
        j = peer_of(k)
        return pltpu.make_async_remote_copy(
            src_ref=fin.at[me], dst_ref=fin.at[me], send_sem=s2.at[k], recv_sem=r2.at[k],
            device_id={"dp": j}, device_id_type=MESH,
        )

    def start1(k, carry):
        scatter(k).start()
        return carry

    def wait1(k, total):
        scatter(k).wait_recv()
        return total + land[k].astype(F32)

    lax.fori_loop(1, n, start1, 0)
    total = lax.fori_loop(1, n, wait1, part[me].astype(F32))
    fin[me] = (total / n).astype(BF16)

    def start2(k, carry):
        spread(k).start()
        return carry

    def wait2(k, carry):
        spread(k).wait_recv()
        return carry

    lax.fori_loop(1, n, start2, 0)
    lax.fori_loop(1, n, wait2, 0)
    for h in range(HH):
        for comp in range(3):
            rows = fin[3 * h + comp].astype(F32)
            stage[0, comp, h] = rows[:8]
            stage[1, comp, h] = rows[8:]
    heads = pl.ds(c * HH, HH)
    cp = pltpu.make_async_remote_copy(
        src_ref=stage.at[other], dst_ref=out.at[:, heads], send_sem=o_ssem, recv_sem=o_rsem,
        device_id={"ctx": partner}, device_id_type=MESH,
    )
    lc = pltpu.make_async_copy(stage.at[c], out.at[:, heads], o_sem)
    cp.start()
    lc.start()

    def wait_sent(k, carry):
        scatter(k).wait_send()
        spread(k).wait_send()
        return carry

    lax.fori_loop(1, n, wait_sent, 0)
    cp.wait()
    lc.wait()


def ring_call(n_ctx, keys_a, values_a, queries_b, grad_out, state_start, state_next):
    tokens = keys_a.shape[1]
    nz = n_ctx // 2
    far = nz // 2
    anyspace = pl.BlockSpec(memory_space=pl.ANY)
    vm = pl.BlockSpec(memory_space=pltpu.VMEM)
    flat = (tokens, H * D)
    dma = pltpu.SemaphoreType.DMA
    rows2 = 2 * tokens
    half = HH * D
    dk, dv, part = pl.pallas_call(
        functools.partial(main_kernel, nz),
        out_shape=(
            jax.ShapeDtypeStruct(flat, BF16),
            jax.ShapeDtypeStruct(flat, BF16),
            jax.ShapeDtypeStruct((32, 16, F), BF16),
        ),
        in_specs=[anyspace] * 6,
        out_specs=(anyspace, anyspace, vm),
        scratch_shapes=[
            pltpu.VMEM((rows2, half), BF16),
            pltpu.VMEM((rows2, half), BF16),
            pltpu.VMEM((rows2, half), BF16),
            pltpu.VMEM((rows2, half), BF16),
            pltpu.VMEM((2, 3, 3, HH, 8, F), F32),
            pltpu.VMEM((HH, D, 3 * F), BF16),
            pltpu.VMEM((HH, D, 3 * F), BF16),
            pltpu.VMEM((32, D, F), BF16),
            pltpu.VMEM((32, D, F), BF16),
            pltpu.VMEM((HH, D, 3 * F), F32),
            pltpu.VMEM((2, 2, far, 4, D, F), BF16),
            pltpu.VMEM((2, 2, far, 4, D, F), BF16),
            pltpu.VMEM((32, D, F), BF16),
            pltpu.VMEM((HH, 3, rows2, F), F32),
            pltpu.VMEM((HH, 3, rows2, F), BF16),
            pltpu.VMEM((rows2, half), BF16),
            pltpu.VMEM((rows2, half), BF16),
            pltpu.VMEM((HH, D, 3 * F), BF16),
            pltpu.VMEM((2, far, HH, 16, 3 * F), BF16),
            pltpu.VMEM((2, far, HH, 16, 3 * F), BF16),
            dma((6,)),
            dma((6,)),
            dma((6,)),
            dma((2, 2, far)),
            dma((2, 2, far)),
            dma((2, 2, far)),
            dma((2, 2, far)),
            dma((2, far)),
            dma((2, far)),
            dma((2, far)),
            dma((2, far)),
            dma((2,)),
            dma((2,)),
            dma((2,)),
        ],
        compiler_params=pltpu.CompilerParams(
            collective_id=0, has_side_effects=True, vmem_limit_bytes=56 * 1024 * 1024
        ),
        name="ttt_ring",
    )(
        keys_a.reshape(flat),
        values_a.reshape(flat),
        queries_b.reshape(flat),
        grad_out.reshape(flat),
        state_start,
        state_next[0],
    )
    return dk, dv, part


def dp_call(n_dp, part):
    anyspace = pl.BlockSpec(memory_space=pl.ANY)
    vm = pl.BlockSpec(memory_space=pltpu.VMEM)
    dma = pltpu.SemaphoreType.DMA
    return pl.pallas_call(
        functools.partial(dp_kernel, n_dp),
        out_shape=jax.ShapeDtypeStruct((3, H, 8, F), F32),
        in_specs=[vm],
        out_specs=anyspace,
        scratch_shapes=[
            pltpu.VMEM((32, 16, F), BF16),
            pltpu.VMEM((32, 16, F), BF16),
            pltpu.VMEM((2, 3, HH, 8, F), F32),
            dma((n_dp,)),
            dma((n_dp,)),
            dma((n_dp,)),
            dma((n_dp,)),
            dma,
            dma,
            dma,
        ],
        compiler_params=pltpu.CompilerParams(collective_id=1, has_side_effects=True),
        name="dp_sum",
    )(part)


def local(n_dp, n_ctx, keys_a, *rest):
    dk, dv, part = ring_call(n_ctx, keys_a, *rest)
    grad_state = dp_call(n_dp, part)
    return dk.reshape(keys_a.shape), dv.reshape(keys_a.shape), grad_state


def solution(mesh):
    placed = (
        P("dp", "ctx", None),
        P("dp", "ctx", None),
        P("dp", "ctx", None),
        P("dp", "ctx", None),
        P(None, None, "ctx", None),
        P("dp", None, None, "ctx", None),
    )
    return jax.shard_map(
        functools.partial(local, mesh.shape["dp"], mesh.shape["ctx"]),
        mesh=mesh,
        in_specs=placed,
        out_specs=(P("dp", "ctx", None), P("dp", "ctx", None), P(None, None, "ctx", None)),
        check_vma=False,
    )
```

```python
import functools

import jax
import jax.numpy as jnp
from jax import lax
from jax.experimental import pallas as pl
from jax.experimental.pallas import tpu as pltpu
from jax.sharding import PartitionSpec as P

D = 128
H = 20
F = 128
HH = H // 2
RATE = 4.0
CA = 3.4445
CB = -4.775
CC = 2.0315
MESH = pl.DeviceIdType.MESH
F32 = jnp.float32
BF16 = jnp.bfloat16


def mm(a, b):
    return jnp.dot(a, b, preferred_element_type=F32)


def mm_tn(a, b):
    return lax.dot_general(a, b, (((0,), (0,)), ((), ())), preferred_element_type=F32)


def mm_nt(a, b):
    return lax.dot_general(a, b, (((1,), (1,)), ((), ())), preferred_element_type=F32)


def newton_forward(mats):
    norms, units, xs, grams, polys = [], [], [], [], []
    for g in mats:
        total = jnp.sum(jnp.sum(g * g, axis=1, keepdims=True), axis=0, keepdims=True)
        n = jnp.sqrt(total + 1e-06)
        u = g / n
        norms.append(n)
        units.append(u)
    x = [u.astype(BF16) for u in units]
    for step in range(2):
        a = [mm_nt(v, v).astype(BF16) for v in x]
        sq = [mm(v, v) for v in a]
        p = [(CB * v.astype(F32) + CC * w).astype(BF16) for v, w in zip(a, sq)]
        xs.append(x)
        grams.append(a)
        polys.append(p)
        if step == 0:
            mixed = [mm(v, w) for v, w in zip(p, x)]
            x = [(CA * v.astype(F32) + w).astype(BF16) for v, w in zip(x, mixed)]
    return norms, units, xs, grams, polys


def newton_backward(saved, cts):
    norms, units, xs, grams, polys = saved
    ct = cts
    for step in (1, 0):
        x, a, p = xs[step], grams[step], polys[step]
        ct_z = [mm_nt(v, w).astype(BF16) for v, w in zip(ct, x)]
        direct = [CA * v.astype(F32) + mm(w, v) for v, w in zip(ct, p)]
        ct_a = [
            (CB * v.astype(F32) + CC * (mm(v, w) + mm(w, v))).astype(BF16)
            for v, w in zip(ct_z, a)
        ]
        ct = [
            (d + mm(v, w) + mm_tn(v, w)).astype(BF16) for d, v, w in zip(direct, ct_a, x)
        ]
    out = []
    for n, u, v in zip(norms, units, ct):
        v = v.astype(F32)
        dot = jnp.sum(jnp.sum(v * u, axis=1, keepdims=True), axis=0, keepdims=True)
        out.append((v - u * dot) / n)
    return out


NX = 4
PARTS = 4


def main_kernel(
    nz, ny, n_dp, merged,
    keys, values, queries, gout, start, nxt,
    *refs,
):
    if merged:
        dk_out, dv_out, grad_out = refs[:3]
        refs = refs[3:]
        dp_refs, refs = refs[:11], refs[11:]
        part = dp_refs[0]
    else:
        dk_out, dv_out, part = refs[:3]
        refs = refs[3:]
    (
        xk, xv, xq, xo, stage, ws, wn, gbuf, sbuf, psum,
        rs_send, rs_recv, field, act, rnd, dk, dv, tot, gr_send, gr_recv,
        in_sem, x_ssem, x_rsem, st_ssem, st_rsem, sx_ssem, sx_rsem, ag_ssem, ag_rsem,
        rs_ssem, rs_rsem, f_ssem, f_rsem, gr_ssem, gr_rsem, o_sem, o_ssem, o_rsem,
    ) = refs
    ctx = lax.axis_index("ctx")
    z = lax.div(ctx, 2)
    c = lax.rem(ctx, 2)
    other = 1 - c
    me = lax.axis_index("dp")
    xi = lax.div(me, ny)
    yi = lax.rem(me, ny)

    def chip(offset):
        return lax.rem(z + offset + 2 * nz, nz)

    def xpos(offset):
        return lax.rem(xi + offset + 2 * NX, NX)

    right = {"ctx": 2 * chip(1) + c}
    left = {"ctx": 2 * chip(-1) + c}
    partner = {"ctx": 2 * z + other}
    xright = {"dp": xpos(1) * ny + yi}
    xleft = {"dp": xpos(-1) * ny + yi}
    half = HH * D
    dirs = ((right, 1), (left, -1))
    xdirs = ((xright, 1), (xleft, -1))
    far = nz // 2

    own_heads = pl.ds(c * HH, HH)
    other_heads = pl.ds(other * HH, HH)
    own_cols = pl.ds(pl.multiple_of(c * half, 128), half)
    other_cols = pl.ds(pl.multiple_of(other * half, 128), half)
    tokens = keys.shape[0]

    locals_in = []
    for k, st in enumerate((start, nxt)):
        lc = pltpu.make_async_copy(
            st.at[:, own_heads], stage.at[k, c, :, pl.ds(0, HH)], in_sem.at[k]
        )
        lc.start()
        locals_in.append(lc)
    token_pairs = ((queries, xq), (gout, xo), (keys, xk), (values, xv))
    for k, (src, dst) in enumerate(token_pairs):
        lc = pltpu.make_async_copy(src.at[:, own_cols], dst.at[0:tokens], in_sem.at[2 + k])
        lc.start()
        locals_in.append(lc)

    barrier = pltpu.get_barrier_semaphore()
    near = [right, left, partner]
    if not merged:
        near = near + [xright, xleft]
    for peer in near:
        pl.semaphore_signal(barrier, inc=1, device_id=peer, device_id_type=MESH)
    if merged:

        def greet(k, carry):
            pl.semaphore_signal(
                barrier, inc=1, device_id={"dp": lax.rem(me + k, n_dp)}, device_id_type=MESH
            )
            return carry

        lax.fori_loop(1, n_dp, greet, 0)
        pl.semaphore_wait(barrier, len(near) + n_dp - 1)
    else:
        pl.semaphore_wait(barrier, len(near))

    sends = []

    def remote(src, dst, ssem, rsem, peer):
        cp = pltpu.make_async_remote_copy(
            src_ref=src, dst_ref=dst, send_sem=ssem, recv_sem=rsem,
            device_id=peer, device_id_type=MESH,
        )
        cp.start()
        sends.append(cp)
        return cp

    remotes_in = []
    for k, st in enumerate((start, nxt)):
        remotes_in.append(
            remote(
                st.at[:, other_heads], stage.at[k, c, :, pl.ds(0, HH)],
                x_ssem.at[k], x_rsem.at[k], partner,
            )
        )
    for k, (src, dst) in enumerate(token_pairs):
        remotes_in.append(
            remote(
                src.at[:, other_cols], dst.at[tokens : 2 * tokens],
                x_ssem.at[2 + k], x_rsem.at[2 + k], partner,
            )
        )

    def rows_of(offset):
        return pl.ds(pl.multiple_of(16 * chip(offset), 16), 16)

    for cc in range(2):
        for comp in range(3):
            stage[0, cc, comp, HH] = jnp.zeros((8, F), F32)
    locals_in[0].wait()
    remotes_in[0].wait_recv()
    quarter = pl.multiple_of(8 * xi, 8)
    for i in range(8):
        m = quarter + i
        h, comp = lax.div(m, 3), lax.rem(m, 3)
        ws[m, rows_of(0), :] = jnp.concatenate(
            [stage[0, 0, comp, h], stage[0, 1, comp, h]], axis=0
        ).astype(BF16)

    counts = [8, 8, 8, 3 * HH - 24]

    def span(cnt, dr, last):
        if not last:
            return 0, cnt
        return (0, cnt // 2) if dr == 0 else (cnt // 2, cnt - cnt // 2)

    ag = {}

    def gather_step(unit, step):
        for dr, (peer, sign) in enumerate(dirs):
            if step > 1:
                ag[unit, dr, step - 1].wait_recv()
            if unit == 0:
                ref, base, cnt = ws, quarter, 8
                sems = st_ssem.at[dr, step - 1], st_rsem.at[dr, step - 1]
            else:
                ref, base, cnt = wn, 8 * (unit - 1), counts[unit - 1]
                sems = ag_ssem.at[unit - 1, dr, step - 1], ag_rsem.at[unit - 1, dr, step - 1]
            lo, n = span(cnt, dr, step == far)
            piece = ref.at[pl.ds(base + lo, n), rows_of(-sign * (step - 1)), :]
            ag[unit, dr, step] = remote(piece, piece, sems[0], sems[1], peer)

    gather_step(0, 1)
    locals_in[1].wait()
    remotes_in[1].wait_recv()
    for p in range(PARTS):
        for i in range(counts[p]):
            m = 8 * p + i
            h, comp = m // 3, m % 3
            wn[m, rows_of(0), :] = jnp.concatenate(
                [stage[1, 0, comp, h], stage[1, 1, comp, h]], axis=0
            ).astype(BF16)
        gather_step(1 + p, 1)
    for step in range(2, far + 1):
        for unit in range(1 + PARTS):
            gather_step(unit, step)

    sx = {}

    def xgather(i, step):
        for dr, (peer, sign) in enumerate(xdirs):
            lo, n = 4 * i, 4
            if step == 2:
                sx[i, dr, 1].wait_recv()
                lo, n = (4 * i, 2) if dr == 0 else (4 * i + 2, 2)
            base = pl.multiple_of(8 * xpos(-sign * (step - 1)), 8)
            piece = ws.at[pl.ds(base + lo, n)]
            sx[i, dr, step] = remote(
                piece, piece, sx_ssem.at[i, dr, step - 1], sx_rsem.at[i, dr, step - 1], peer
            )

    ag[0, 0, far].wait_recv()
    ag[0, 1, far].wait_recv()
    xgather(0, 1)
    xgather(1, 1)

    def phi(h, xs, ys, w):
        cols = pl.ds(pl.multiple_of(h * D, 128), D)
        x, y = xs[:, cols], ys[:, cols]
        gu = mm(x, jnp.concatenate([w[3 * h], w[3 * h + 1]], axis=1))
        proj = mm(y, w[3 * h + 2])
        gate, up = gu[:, :F], gu[:, F:]
        s = jax.nn.sigmoid(gate)
        swish = gate * s
        hidden = (swish * up).astype(BF16)
        d_gate = (proj * up * s * (1.0 + gate * (1.0 - s))).astype(BF16)
        d_up = (proj * swish).astype(BF16)
        gab = mm_tn(x, jnp.concatenate([d_gate, d_up], axis=1))
        gc = mm_tn(y, hidden)
        return gate, up, proj, hidden, d_gate, d_up, (gab[:, :F], gab[:, F:], gc)

    def phi_a(h, carry):
        gate, up, proj, hidden, d_gate, d_up, grads = phi(h, xk, xv, ws)
        act[h, 0] = gate
        act[h, 1] = up
        act[h, 2] = proj
        rnd[h, 0] = d_gate
        rnd[h, 1] = d_up
        rnd[h, 2] = hidden
        for i in range(3):
            gbuf[3 * h + i] = grads[i].astype(BF16)
        return carry

    def phi_b(h, carry):
        grads = phi(h, xq, xo, wn)[-1]
        for i in range(3):
            psum[3 * h + i] = grads[i]
            sbuf[3 * h + i] = grads[i].astype(BF16)
        return carry

    for pad in (3 * HH, 3 * HH + 1):
        gbuf[pad] = jnp.zeros((D, F), BF16)
        sbuf[pad] = jnp.zeros((D, F), BF16)

    bufs = (gbuf, sbuf)
    rs = {}
    rows_half = D // 2

    def rs_step(k, p, step):
        for dr, (peer, sign) in enumerate(dirs):
            slot = 8 * p + chip(sign * (far + 1 - step))
            lo, n = (0, D)
            if step == 1:
                lo, n = (0, rows_half) if dr == 0 else (rows_half, rows_half)
                src = bufs[k].at[slot, pl.ds(lo, n)]
            else:
                rs[k, p, dr, step - 1].wait_recv()
                if step == 2:
                    a = 0 if dr == 0 else rows_half
                    b = rows_half - a
                    part_sum = bufs[k][slot, a : a + rows_half].astype(F32) + rs_recv[
                        k, p, dr, 0, a : a + rows_half
                    ].astype(F32)
                    rs_send[k, p, dr, 0, a : a + rows_half] = part_sum.astype(BF16)
                    rs_send[k, p, dr, 0, b : b + rows_half] = bufs[k][slot, b : b + rows_half]
                else:
                    total = bufs[k][slot].astype(F32) + rs_recv[k, p, dr, step - 2].astype(F32)
                    rs_send[k, p, dr, step - 2] = total.astype(BF16)
                src = rs_send.at[k, p, dr, step - 2]
            dst = rs_recv.at[k, p, dr, step - 1, pl.ds(lo, n)]
            rs[k, p, dr, step] = remote(
                src, dst, rs_ssem.at[k, p, dr, step - 1], rs_rsem.at[k, p, dr, step - 1], peer
            )

    def rs_total(k):
        out = []
        for p in range(PARTS):
            v = bufs[k][8 * p + z].astype(F32)
            for dr in range(2):
                rs[k, p, dr, far].wait_recv()
                v = v + rs_recv[k, p, dr, far - 1].astype(F32)
            out.append(v)
        return out

    groups = ((0, 3), (3, 6), (6, 8), (8, HH))
    for k in range(2):
        locals_in[2 + k].wait()
        remotes_in[2 + k].wait_recv()
    for p in range(PARTS):
        for unit in ((1, 2), (3,), (), (4,))[p]:
            ag[unit, 0, far].wait_recv()
            ag[unit, 1, far].wait_recv()
        lax.fori_loop(groups[p][0], groups[p][1], phi_b, 0)
        rs_step(1, p, 1)
    xgather(0, 2)
    for p in range(PARTS):
        rs_step(1, p, 2)
    xgather(1, 2)
    for step in range(3, far + 1):
        for p in range(PARTS):
            rs_step(1, p, step)
    for i in range(2):
        sx[i, 0, 2].wait_recv()
        sx[i, 1, 2].wait_recv()
    for k in range(2):
        locals_in[4 + k].wait()
        remotes_in[4 + k].wait_recv()
    for p in range(PARTS):
        lax.fori_loop(groups[p][0], groups[p][1], phi_a, 0)
        rs_step(0, p, 1)
    cts = [(RATE * v).astype(BF16) for v in rs_total(1)]
    for step in range(2, far + 1):
        for p in range(PARTS):
            rs_step(0, p, step)
    saved = newton_forward(rs_total(0))
    fields = newton_backward(saved, cts)

    fd = {}

    def field_step(p, step):
        for dr, (peer, sign) in enumerate(dirs):
            if step > 1:
                fd[p, dr, step - 1].wait_recv()
            lo, n = span(D, dr, step == far)
            piece = field.at[8 * p + chip(-sign * (step - 1)), pl.ds(lo, n)]
            fd[p, dr, step] = remote(
                piece, piece, f_ssem.at[p, dr, step - 1], f_rsem.at[p, dr, step - 1], peer
            )

    for p in range(PARTS):
        field[8 * p + z] = fields[p].astype(BF16)
        field_step(p, 1)
    for step in range(2, far + 1):
        for p in range(PARTS):
            field_step(p, step)

    def back(h, carry):
        cols = pl.ds(pl.multiple_of(h * D, 128), D)
        x, y = xk[:, cols], xv[:, cols]
        gate, up, proj = act[h, 0], act[h, 1], act[h, 2]
        d_gate, d_up, hidden = rnd[h, 0], rnd[h, 1], rnd[h, 2]
        da, db, dc = field[3 * h], field[3 * h + 1], field[3 * h + 2]
        dab = jnp.concatenate([da, db], axis=1)
        ct_gu = mm(x, dab).astype(BF16).astype(F32)
        ct_dg, ct_du = ct_gu[:, :F], ct_gu[:, F:]
        ct_h = mm(y, dc).astype(BF16).astype(F32)
        s = jax.nn.sigmoid(gate)
        swish = gate * s
        sd = s * (1.0 - s)
        q = s + gate * sd
        qd = sd * (2.0 + gate * (1.0 - 2.0 * s))
        ct_w = ct_h * up + ct_du * proj
        cq = ct_dg * q
        ct_up = (ct_h * swish + cq * proj).astype(BF16)
        ct_p = (ct_du * swish + cq * up).astype(BF16)
        ct_gate = (ct_w * q + ct_dg * (proj * up) * qd).astype(BF16)
        wab = jnp.concatenate([ws[3 * h], ws[3 * h + 1]], axis=1)
        ct_ab = jnp.concatenate([ct_gate, ct_up], axis=1)
        d_ab = jnp.concatenate([d_gate, d_up], axis=1)
        dx = mm_nt(d_ab, dab) + mm_nt(ct_ab, wab)
        dy = mm_nt(hidden, dc) + mm_nt(ct_p, ws[3 * h + 2])
        dk[:, cols] = dx.astype(BF16)
        dv[:, cols] = dy.astype(BF16)
        wg = mm_tn(x, ct_ab)
        tot[3 * h] = (psum[3 * h] + wg[:, :F]).astype(BF16)
        tot[3 * h + 1] = (psum[3 * h + 1] + wg[:, F:]).astype(BF16)
        tot[3 * h + 2] = (psum[3 * h + 2] + mm_tn(y, ct_p)).astype(BF16)
        return carry

    gr = {}

    def grad_step(p, step):
        cnt = counts[p]
        for dr, (peer, sign) in enumerate(dirs):
            rows = rows_of(sign * (far + 1 - step))
            lo, n = span(cnt, dr, step == 1)
            if step == 1:
                src = tot.at[pl.ds(8 * p + lo, n), rows, :]
            else:
                gr[p, dr, step - 1].wait_recv()
                if step == 2:
                    a, na = span(cnt, dr, True)
                    b, nb = span(cnt, 1 - dr, True)
                    own = tot[8 * p + a : 8 * p + a + na, rows, :].astype(F32)
                    own = own + gr_recv[p, dr, 0, a : a + na].astype(F32)
                    gr_send[p, dr, 0, a : a + na] = own.astype(BF16)
                    gr_send[p, dr, 0, b : b + nb] = tot[8 * p + b : 8 * p + b + nb, rows, :]
                else:
                    own = tot[8 * p : 8 * p + cnt, rows, :].astype(F32)
                    own = own + gr_recv[p, dr, step - 2, :cnt].astype(F32)
                    gr_send[p, dr, step - 2, :cnt] = own.astype(BF16)
                src = gr_send.at[p, dr, step - 2, pl.ds(0, cnt)]
            dst = gr_recv.at[p, dr, step - 1, pl.ds(lo, n)]
            gr[p, dr, step] = remote(
                src, dst, gr_ssem.at[p, dr, step - 1], gr_rsem.at[p, dr, step - 1], peer
            )

    for p in range(PARTS):
        for unit in ((0, 1), (2,), (), (3,))[p]:
            fd[unit, 0, far].wait_recv()
            fd[unit, 1, far].wait_recv()
        lax.fori_loop(groups[p][0], groups[p][1], back, 0)
        grad_step(p, 1)

    outs = []
    for k, (src, dst) in enumerate(((dk, dk_out), (dv, dv_out))):
        cp = remote(
            src.at[tokens : 2 * tokens], dst.at[:, own_cols], o_ssem.at[k], o_rsem.at[k], partner
        )
        lc = pltpu.make_async_copy(src.at[0:tokens], dst.at[:, own_cols], o_sem.at[k])
        lc.start()
        outs.append((cp, lc))

    for step in range(2, far + 1):
        for p in range(PARTS):
            grad_step(p, step)
    for p in range(PARTS):
        cnt = counts[p]
        own = tot[8 * p : 8 * p + cnt, rows_of(0), :].astype(F32)
        for dr in range(2):
            gr[p, dr, far].wait_recv()
            own = own + gr_recv[p, dr, far - 1, :cnt].astype(F32)
        part[8 * p : 8 * p + cnt] = own.astype(BF16)
    part[3 * HH :] = jnp.zeros((32 - 3 * HH, 16, F), BF16)
    if merged:
        dp_phase(n_dp, grad_out, *dp_refs)

    for cp in sends:
        cp.wait_send()
    for cp, lc in outs:
        cp.wait_recv()
        lc.wait()


def dp_phase(n, out, part, land, fin, rowbuf, swap, s1, r1, s2, r2, c_ssem, c_rsem):
    ctx = lax.axis_index("ctx")
    c = lax.rem(ctx, 2)
    other = 1 - c
    partner = ctx + 1 - 2 * c
    me = lax.axis_index("dp")
    per = 32 // n

    def scatter(k):
        j = lax.rem(me + k, n)
        return pltpu.make_async_remote_copy(
            src_ref=part.at[pl.ds(per * j, per)], dst_ref=land.at[k],
            send_sem=s1.at[k], recv_sem=r1.at[k],
            device_id={"dp": j}, device_id_type=MESH,
        )

    def spread(k):
        j = lax.rem(me + k, n)
        mine = fin.at[pl.ds(per * me, per)]
        return pltpu.make_async_remote_copy(
            src_ref=mine, dst_ref=mine, send_sem=s2.at[k], recv_sem=r2.at[k],
            device_id={"dp": j}, device_id_type=MESH,
        )

    def start1(k, carry):
        scatter(k).start()
        return carry

    def wait1(k, total):
        scatter(k).wait_recv()
        return total + land[k].astype(F32)

    lax.fori_loop(1, n, start1, 0)
    total = lax.fori_loop(1, n, wait1, part[pl.ds(per * me, per)].astype(F32)) / n
    rowbuf[0] = total[:, :8]
    rowbuf[1] = total[:, 8:]
    cp = pltpu.make_async_remote_copy(
        src_ref=rowbuf.at[other], dst_ref=swap.at[c], send_sem=c_ssem, recv_sem=c_rsem,
        device_id={"ctx": partner}, device_id_type=MESH,
    )
    cp.start()
    swap[c] = rowbuf[c]
    cp.wait_recv()
    fin[pl.ds(per * me, per)] = jnp.concatenate([swap[0], swap[1]], axis=1).astype(BF16)

    def start2(k, carry):
        spread(k).start()
        return carry

    def wait2(k, carry):
        spread(k).wait_recv()
        return carry

    lax.fori_loop(1, n, start2, 0)
    lax.fori_loop(1, n, wait2, 0)
    for h in range(HH):
        for comp in range(3):
            rows = fin[3 * h + comp].astype(F32)
            out[comp, h] = rows[:8]
            out[comp, HH + h] = rows[8:]

    def wait_sent(k, carry):
        scatter(k).wait_send()
        spread(k).wait_send()
        return carry

    lax.fori_loop(1, n, wait_sent, 0)
    cp.wait_send()


def dp_kernel(n, part, out, *refs):
    ctx = lax.axis_index("ctx")
    partner = ctx + 1 - 2 * lax.rem(ctx, 2)
    me = lax.axis_index("dp")
    barrier = pltpu.get_barrier_semaphore()

    def greet(k, carry):
        pl.semaphore_signal(
            barrier, inc=1, device_id={"dp": lax.rem(me + k, n)}, device_id_type=MESH
        )
        return carry

    lax.fori_loop(1, n, greet, 0)
    pl.semaphore_signal(barrier, inc=1, device_id={"ctx": partner}, device_id_type=MESH)
    pl.semaphore_wait(barrier, n)
    dp_phase(n, out, part, *refs)


def land_kernel(dk, dv, gs, dk_out, dv_out, gs_out, sems):
    copies = []
    for i, (src, dst) in enumerate(((dk, dk_out), (dv, dv_out), (gs, gs_out))):
        cp = pltpu.make_async_copy(src, dst, sems.at[i])
        cp.start()
        copies.append(cp)
    for cp in copies:
        cp.wait()


def dp_scratch(n_dp):
    dma = pltpu.SemaphoreType.DMA
    per = 32 // n_dp
    return [
        pltpu.VMEM((n_dp, per, 16, F), BF16),
        pltpu.VMEM((32, 16, F), BF16),
        pltpu.VMEM((2, per, 8, F), F32),
        pltpu.VMEM((2, per, 8, F), F32),
        dma((n_dp,)),
        dma((n_dp,)),
        dma((n_dp,)),
        dma((n_dp,)),
        dma,
        dma,
    ]


def run(n_dp, n_ctx, merged, keys_a, values_a, queries_b, grad_out, state_start, state_next):
    tokens = keys_a.shape[1]
    nz = n_ctx // 2
    far = nz // 2
    anyspace = pl.BlockSpec(memory_space=pl.ANY)
    vm = pl.BlockSpec(memory_space=pltpu.VMEM)
    flat = (tokens, H * D)
    dma = pltpu.SemaphoreType.DMA
    rows2 = 2 * tokens
    half = HH * D
    token_buf = pltpu.VMEM((rows2, half), BF16)
    mats = pltpu.VMEM((32, D, F), BF16)
    grad_shape = jax.ShapeDtypeStruct((3, H, 8, F), F32)
    part_shape = jax.ShapeDtypeStruct((32, 16, F), BF16)
    dp_list = dp_scratch(n_dp)
    ring_sems = [dma((PARTS, 2, far)), dma((PARTS, 2, far))]
    outs = pl.pallas_call(
        functools.partial(main_kernel, nz, n_dp // NX, n_dp, merged),
        out_shape=(
            jax.ShapeDtypeStruct(flat, BF16),
            jax.ShapeDtypeStruct(flat, BF16),
            grad_shape if merged else part_shape,
        ),
        in_specs=[pl.BlockSpec(memory_space=pltpu.HBM)] * 6,
        out_specs=(OUT_SPACE, OUT_SPACE, vm),
        scratch_shapes=([pltpu.VMEM((32, 16, F), BF16)] + dp_list if merged else [])
        + [
            token_buf, token_buf, token_buf, token_buf,
            pltpu.VMEM((2, 2, 3, HH + 1, 8, F), F32),
            mats, mats, mats, mats,
            pltpu.VMEM((3 * HH, D, F), F32),
            pltpu.VMEM((2, PARTS, 2, far - 1, D, F), BF16),
            pltpu.VMEM((2, PARTS, 2, far, D, F), BF16),
            mats,
            pltpu.VMEM((HH, 3, rows2, F), F32),
            pltpu.VMEM((HH, 3, rows2, F), BF16),
            token_buf, token_buf,
            mats,
            pltpu.VMEM((PARTS, 2, far - 1, 8, 16, F), BF16),
            pltpu.VMEM((PARTS, 2, far, 8, 16, F), BF16),
            dma((6,)), dma((6,)), dma((6,)),
            dma((2, far)), dma((2, far)),
            dma((2, 2, 2)), dma((2, 2, 2)),
        ]
        + ring_sems
        + [dma((2, PARTS, 2, far)), dma((2, PARTS, 2, far))]
        + ring_sems
        + ring_sems
        + [dma((2,)), dma((2,)), dma((2,))],
        compiler_params=pltpu.CompilerParams(
            collective_id=0, has_side_effects=True, vmem_limit_bytes=RING_VMEM
        ),
        name="ttt_ring",
    )(
        keys_a.reshape(flat),
        values_a.reshape(flat),
        queries_b.reshape(flat),
        grad_out.reshape(flat),
        state_start,
        state_next[0],
    )
    if merged:
        dk, dv, gs = outs
    else:
        dk, dv, part = outs
        gs = pl.pallas_call(
            functools.partial(dp_kernel, n_dp),
            out_shape=grad_shape,
            in_specs=[vm],
            out_specs=vm,
            scratch_shapes=dp_list,
            compiler_params=pltpu.CompilerParams(
                collective_id=1, has_side_effects=True, vmem_limit_bytes=4 * 1024 * 1024
            ),
            name="dp_sum",
        )(part)
    dk, dv, gs = pl.pallas_call(
        land_kernel,
        out_shape=(
            jax.ShapeDtypeStruct(flat, BF16),
            jax.ShapeDtypeStruct(flat, BF16),
            grad_shape,
        ),
        in_specs=[vm] * 3,
        out_specs=(anyspace,) * 3,
        scratch_shapes=[dma((3,))],
        compiler_params=pltpu.CompilerParams(vmem_limit_bytes=8 * 1024 * 1024),
        name="land",
    )(dk, dv, gs)
    return dk.reshape(keys_a.shape), dv.reshape(keys_a.shape), gs


MERGED = True
OUT_SPACE = pl.BlockSpec(memory_space=pltpu.VMEM)
RING_VMEM = 53000 * 1024


def solution(mesh):
    placed = (
        P("dp", "ctx", None),
        P("dp", "ctx", None),
        P("dp", "ctx", None),
        P("dp", "ctx", None),
        P(None, None, "ctx", None),
        P("dp", None, None, "ctx", None),
    )
    return jax.shard_map(
        functools.partial(run, mesh.shape["dp"], mesh.shape["ctx"], MERGED),
        mesh=mesh,
        in_specs=placed,
        out_specs=(P("dp", "ctx", None), P("dp", "ctx", None), P(None, None, "ctx", None)),
        check_vma=False,
    )
```

```python
import functools

import jax
import jax.numpy as jnp
from jax import lax
from jax.experimental import pallas as pl
from jax.experimental.pallas import tpu as pltpu
from jax.sharding import PartitionSpec as P

D = 128
H = 20
F = 128
HH = H // 2
RATE = 4.0
CA = 3.4445
CB = -4.775
CC = 2.0315
MESH = pl.DeviceIdType.MESH
F32 = jnp.float32
BF16 = jnp.bfloat16


def mm(a, b):
    return jnp.dot(a, b, preferred_element_type=F32)


def mm_tn(a, b):
    return lax.dot_general(a, b, (((0,), (0,)), ((), ())), preferred_element_type=F32)


def mm_nt(a, b):
    return lax.dot_general(a, b, (((1,), (1,)), ((), ())), preferred_element_type=F32)


def newton_forward(mats):
    norms, units, xs, grams, polys = [], [], [], [], []
    for g in mats:
        total = jnp.sum(jnp.sum(g * g, axis=1, keepdims=True), axis=0, keepdims=True)
        n = jnp.sqrt(total + 1e-06)
        u = g / n
        norms.append(n)
        units.append(u)
    x = [u.astype(BF16) for u in units]
    for step in range(2):
        a = [mm_nt(v, v).astype(BF16) for v in x]
        sq = [mm(v, v) for v in a]
        p = [(CB * v.astype(F32) + CC * w).astype(BF16) for v, w in zip(a, sq)]
        xs.append(x)
        grams.append(a)
        polys.append(p)
        if step == 0:
            mixed = [mm(v, w) for v, w in zip(p, x)]
            x = [(CA * v.astype(F32) + w).astype(BF16) for v, w in zip(x, mixed)]
    return norms, units, xs, grams, polys


def newton_backward(saved, cts):
    norms, units, xs, grams, polys = saved
    ct = cts
    for step in (1, 0):
        x, a, p = xs[step], grams[step], polys[step]
        ct_z = [mm_nt(v, w).astype(BF16) for v, w in zip(ct, x)]
        direct = [CA * v.astype(F32) + mm(w, v) for v, w in zip(ct, p)]
        ct_a = [
            (CB * v.astype(F32) + CC * (mm(v, w) + mm(w, v))).astype(BF16)
            for v, w in zip(ct_z, a)
        ]
        ct = [
            (d + mm(v, w) + mm_tn(v, w)).astype(BF16) for d, v, w in zip(direct, ct_a, x)
        ]
    out = []
    for n, u, v in zip(norms, units, ct):
        v = v.astype(F32)
        dot = jnp.sum(jnp.sum(v * u, axis=1, keepdims=True), axis=0, keepdims=True)
        out.append((v - u * dot) / n)
    return out


NX = 4
PARTS = 4


def main_kernel(
    nz, ny, n_dp,
    keys, values, queries, gout, start, nxt,
    *refs,
):
    dk_out, dv_out, grad_out = refs[:3]
    dp_refs, refs = refs[3:10], refs[10:]
    part = dp_refs[0]
    (
        xk, xv, xq, xo, stage, ws, wn, gbuf, sbuf, psum,
        rs_send, rs_recv, field, act, aux, rnd, dk, dv, tot, gr_send, gr_recv,
        in_sem, x_ssem, x_rsem, st_ssem, st_rsem, sx_ssem, sx_rsem, ag_ssem, ag_rsem,
        rs_ssem, rs_rsem, f_ssem, f_rsem, gr_ssem, gr_rsem, o_sem, o_ssem, o_rsem,
    ) = refs
    ctx = lax.axis_index("ctx")
    z = lax.div(ctx, 2)
    c = lax.rem(ctx, 2)
    other = 1 - c
    me = lax.axis_index("dp")
    xi = lax.div(me, ny)
    yi = lax.rem(me, ny)

    def chip(offset):
        return lax.rem(z + offset + 2 * nz, nz)

    def xpos(offset):
        return lax.rem(xi + offset + 2 * NX, NX)

    right = {"ctx": 2 * chip(1) + c}
    left = {"ctx": 2 * chip(-1) + c}
    partner = {"ctx": 2 * z + other}
    xright = {"dp": xpos(1) * ny + yi}
    xleft = {"dp": xpos(-1) * ny + yi}
    half = HH * D
    dirs = ((right, 1), (left, -1))
    xdirs = ((xright, 1), (xleft, -1))
    far = nz // 2

    own_heads = pl.ds(c * HH, HH)
    other_heads = pl.ds(other * HH, HH)
    own_cols = pl.ds(pl.multiple_of(c * half, 128), half)
    other_cols = pl.ds(pl.multiple_of(other * half, 128), half)
    tokens = keys.shape[0]

    locals_in = []
    for k, st in enumerate((start, nxt)):
        lc = pltpu.make_async_copy(
            st.at[:, own_heads], stage.at[k, c, :, pl.ds(0, HH)], in_sem.at[k]
        )
        lc.start()
        locals_in.append(lc)
    token_pairs = ((queries, xq), (gout, xo), (keys, xk), (values, xv))
    for k, (src, dst) in enumerate(token_pairs):
        lc = pltpu.make_async_copy(src.at[:, own_cols], dst.at[0:tokens], in_sem.at[2 + k])
        lc.start()
        locals_in.append(lc)

    barrier = pltpu.get_barrier_semaphore()
    near = (right, left, partner)
    for peer in near:
        pl.semaphore_signal(barrier, inc=1, device_id=peer, device_id_type=MESH)

    def greet(k, carry):
        for r in range(2):
            pl.semaphore_signal(
                barrier, inc=1,
                device_id={"dp": lax.rem(me + k, n_dp), "ctx": 2 * z + r}, device_id_type=MESH,
            )
        return carry

    lax.fori_loop(1, n_dp, greet, 0)
    pl.semaphore_wait(barrier, len(near) + 2 * (n_dp - 1))

    sends = []

    def remote(src, dst, ssem, rsem, peer):
        cp = pltpu.make_async_remote_copy(
            src_ref=src, dst_ref=dst, send_sem=ssem, recv_sem=rsem,
            device_id=peer, device_id_type=MESH,
        )
        cp.start()
        sends.append(cp)
        return cp

    remotes_in = []
    for k, st in enumerate((start, nxt)):
        remotes_in.append(
            remote(
                st.at[:, other_heads], stage.at[k, c, :, pl.ds(0, HH)],
                x_ssem.at[k], x_rsem.at[k], partner,
            )
        )
    for k, (src, dst) in enumerate(token_pairs):
        remotes_in.append(
            remote(
                src.at[:, other_cols], dst.at[tokens : 2 * tokens],
                x_ssem.at[2 + k], x_rsem.at[2 + k], partner,
            )
        )

    def rows_of(offset):
        return pl.ds(pl.multiple_of(16 * chip(offset), 16), 16)

    for cc in range(2):
        for comp in range(3):
            stage[0, cc, comp, HH] = jnp.zeros((8, F), F32)
    locals_in[0].wait()
    remotes_in[0].wait_recv()
    quarter = pl.multiple_of(8 * xi, 8)
    for i in range(8):
        m = quarter + i
        h, comp = lax.div(m, 3), lax.rem(m, 3)
        ws[m, rows_of(0), :] = jnp.concatenate(
            [stage[0, 0, comp, h], stage[0, 1, comp, h]], axis=0
        ).astype(BF16)

    counts = [8, 8, 8, 3 * HH - 24]

    def span(cnt, dr, last):
        if not last:
            return 0, cnt
        return (0, cnt // 2) if dr == 0 else (cnt // 2, cnt - cnt // 2)

    ag = {}

    def gather_step(unit, step):
        for dr, (peer, sign) in enumerate(dirs):
            if step > 1:
                ag[unit, dr, step - 1].wait_recv()
            if unit == 0:
                ref, base, cnt = ws, quarter, 8
                sems = st_ssem.at[dr, step - 1], st_rsem.at[dr, step - 1]
            else:
                ref, base, cnt = wn, 8 * (unit - 1), counts[unit - 1]
                sems = ag_ssem.at[unit - 1, dr, step - 1], ag_rsem.at[unit - 1, dr, step - 1]
            lo, n = span(cnt, dr, step == far)
            piece = ref.at[pl.ds(base + lo, n), rows_of(-sign * (step - 1)), :]
            ag[unit, dr, step] = remote(piece, piece, sems[0], sems[1], peer)

    gather_step(0, 1)
    locals_in[1].wait()
    remotes_in[1].wait_recv()
    for p in range(PARTS):
        for i in range(counts[p]):
            m = 8 * p + i
            h, comp = m // 3, m % 3
            wn[m, rows_of(0), :] = jnp.concatenate(
                [stage[1, 0, comp, h], stage[1, 1, comp, h]], axis=0
            ).astype(BF16)
        gather_step(1 + p, 1)
    for step in range(2, far + 1):
        for unit in range(1 + PARTS):
            gather_step(unit, step)

    sx = {}

    def xgather(i, step):
        for dr, (peer, sign) in enumerate(xdirs):
            lo, n = 4 * i, 4
            if step == 2:
                sx[i, dr, 1].wait_recv()
                lo, n = (4 * i, 2) if dr == 0 else (4 * i + 2, 2)
            base = pl.multiple_of(8 * xpos(-sign * (step - 1)), 8)
            piece = ws.at[pl.ds(base + lo, n)]
            sx[i, dr, step] = remote(
                piece, piece, sx_ssem.at[i, dr, step - 1], sx_rsem.at[i, dr, step - 1], peer
            )

    ag[0, 0, far].wait_recv()
    ag[0, 1, far].wait_recv()
    xgather(0, 1)
    xgather(1, 1)

    def phi(h, xs, ys, w):
        cols = slice(h * D, (h + 1) * D)
        x, y = xs[:, cols], ys[:, cols]
        gu = mm(x, jnp.concatenate([w[3 * h], w[3 * h + 1]], axis=1))
        proj = mm(y, w[3 * h + 2])
        gate, up = gu[:, :F], gu[:, F:]
        s = jax.nn.sigmoid(gate)
        swish = gate * s
        hidden = (swish * up).astype(BF16)
        d_gate = (proj * up * s * (1.0 + gate * (1.0 - s))).astype(BF16)
        d_up = (proj * swish).astype(BF16)
        gab = mm_tn(x, jnp.concatenate([d_gate, d_up], axis=1))
        gc = mm_tn(y, hidden)
        return gate, up, proj, hidden, d_gate, d_up, (gab[:, :F], gab[:, F:], gc)

    def phi_a(h):
        gate, up, proj, hidden, d_gate, d_up, grads = phi(h, xk, xv, ws)
        act[h, 0] = gate
        act[h, 1] = up
        act[h, 2] = proj
        rnd[h, 0] = d_gate
        rnd[h, 1] = d_up
        rnd[h, 2] = hidden
        for i in range(3):
            gbuf[3 * h + i] = grads[i].astype(BF16)

    def phi_b(h):
        grads = phi(h, xq, xo, wn)[-1]
        for i in range(3):
            psum[3 * h + i] = grads[i]
            sbuf[3 * h + i] = grads[i].astype(BF16)

    for pad in (3 * HH, 3 * HH + 1):
        gbuf[pad] = jnp.zeros((D, F), BF16)
        sbuf[pad] = jnp.zeros((D, F), BF16)

    bufs = (gbuf, sbuf)
    rs = {}
    rows_half = D // 2

    def rs_step(k, p, step):
        for dr, (peer, sign) in enumerate(dirs):
            slot = 8 * p + chip(sign * (far + 1 - step))
            lo, n = (0, D)
            if step == 1:
                lo, n = (0, rows_half) if dr == 0 else (rows_half, rows_half)
                src = bufs[k].at[slot, pl.ds(lo, n)]
            else:
                rs[k, p, dr, step - 1].wait_recv()
                if step == 2:
                    a = 0 if dr == 0 else rows_half
                    b = rows_half - a
                    part_sum = bufs[k][slot, a : a + rows_half].astype(F32) + rs_recv[
                        k, p, dr, 0, a : a + rows_half
                    ].astype(F32)
                    rs_send[k, p, dr, 0, a : a + rows_half] = part_sum.astype(BF16)
                    rs_send[k, p, dr, 0, b : b + rows_half] = bufs[k][slot, b : b + rows_half]
                else:
                    total = bufs[k][slot].astype(F32) + rs_recv[k, p, dr, step - 2].astype(F32)
                    rs_send[k, p, dr, step - 2] = total.astype(BF16)
                src = rs_send.at[k, p, dr, step - 2]
            dst = rs_recv.at[k, p, dr, step - 1, pl.ds(lo, n)]
            rs[k, p, dr, step] = remote(
                src, dst, rs_ssem.at[k, p, dr, step - 1], rs_rsem.at[k, p, dr, step - 1], peer
            )

    def rs_total(k, parts):
        out = []
        for p in parts:
            v = bufs[k][8 * p + z].astype(F32)
            for dr in range(2):
                rs[k, p, dr, far].wait_recv()
                v = v + rs_recv[k, p, dr, far - 1].astype(F32)
            out.append(v)
        return out

    groups = ((0, 3), (3, 6), (6, 8), (8, HH))
    for k in range(2):
        locals_in[2 + k].wait()
        remotes_in[2 + k].wait_recv()
    for p in range(PARTS):
        for unit in ((1, 2), (3,), (), (4,))[p]:
            ag[unit, 0, far].wait_recv()
            ag[unit, 1, far].wait_recv()
        for h in range(groups[p][0], groups[p][1]):
            phi_b(h)
        rs_step(1, p, 1)
    xgather(0, 2)
    for p in range(PARTS):
        rs_step(1, p, 2)
    xgather(1, 2)
    for step in range(3, far + 1):
        for p in range(PARTS):
            rs_step(1, p, step)
    for i in range(2):
        sx[i, 0, 2].wait_recv()
        sx[i, 1, 2].wait_recv()
    for k in range(2):
        locals_in[4 + k].wait()
        remotes_in[4 + k].wait_recv()
    for p in range(PARTS):
        for h in range(groups[p][0], groups[p][1]):
            phi_a(h)
        rs_step(0, p, 1)
    cts = [(RATE * v).astype(BF16) for v in rs_total(1, range(PARTS))]
    for step in range(2, far + 1):
        for p in range(PARTS):
            rs_step(0, p, step)
    fd = {}

    def field_step(p, step):
        for dr, (peer, sign) in enumerate(dirs):
            if step > 1:
                fd[p, dr, step - 1].wait_recv()
            lo, n = span(D, dr, step == far)
            piece = field.at[8 * p + chip(-sign * (step - 1)), pl.ds(lo, n)]
            fd[p, dr, step] = remote(
                piece, piece, f_ssem.at[p, dr, step - 1], f_rsem.at[p, dr, step - 1], peer
            )

    for pair in ((0, 1), (2, 3)):
        saved = newton_forward(rs_total(0, pair))
        fields = newton_backward(saved, [cts[p] for p in pair])
        for p, value in zip(pair, fields):
            field[8 * p + z] = value.astype(BF16)
            field_step(p, 1)

    def ready(h):
        gate, up, proj = act[h, 0], act[h, 1], act[h, 2]
        s = jax.nn.sigmoid(gate)
        sd = s * (1.0 - s)
        aux[h, 0] = gate * s
        aux[h, 1] = s + gate * sd
        aux[h, 2] = (proj * up) * (sd * (2.0 + gate * (1.0 - 2.0 * s)))

    for step in range(2, far + 1):
        for h in range(HH * (step - 2) // (far - 1), HH * (step - 1) // (far - 1)):
            ready(h)
        for p in range(PARTS):
            field_step(p, step)

    def back(h):
        cols = slice(h * D, (h + 1) * D)
        x, y = xk[:, cols], xv[:, cols]
        up, proj = act[h, 1], act[h, 2]
        swish, q, bend = aux[h, 0], aux[h, 1], aux[h, 2]
        d_gate, d_up, hidden = rnd[h, 0], rnd[h, 1], rnd[h, 2]
        da, db, dc = field[3 * h], field[3 * h + 1], field[3 * h + 2]
        dab = jnp.concatenate([da, db], axis=1)
        ct_gu = mm(x, dab).astype(BF16).astype(F32)
        ct_dg, ct_du = ct_gu[:, :F], ct_gu[:, F:]
        ct_h = mm(y, dc).astype(BF16).astype(F32)
        ct_w = ct_h * up + ct_du * proj
        cq = ct_dg * q
        ct_up = (ct_h * swish + cq * proj).astype(BF16)
        ct_p = (ct_du * swish + cq * up).astype(BF16)
        ct_gate = (ct_w * q + ct_dg * bend).astype(BF16)
        wab = jnp.concatenate([ws[3 * h], ws[3 * h + 1]], axis=1)
        ct_ab = jnp.concatenate([ct_gate, ct_up], axis=1)
        d_ab = jnp.concatenate([d_gate, d_up], axis=1)
        dx = mm_nt(d_ab, dab) + mm_nt(ct_ab, wab)
        dy = mm_nt(hidden, dc) + mm_nt(ct_p, ws[3 * h + 2])
        dk[:, cols] = dx.astype(BF16)
        dv[:, cols] = dy.astype(BF16)
        wg = mm_tn(x, ct_ab)
        tot[3 * h] = (psum[3 * h] + wg[:, :F]).astype(BF16)
        tot[3 * h + 1] = (psum[3 * h + 1] + wg[:, F:]).astype(BF16)
        tot[3 * h + 2] = (psum[3 * h + 2] + mm_tn(y, ct_p)).astype(BF16)

    gr = {}

    def grad_step(p, step):
        cnt = counts[p]
        for dr, (peer, sign) in enumerate(dirs):
            rows = rows_of(sign * (far + 1 - step))
            lo, n = span(cnt, dr, step == 1)
            if step == 1:
                src = tot.at[pl.ds(8 * p + lo, n), rows, :]
            else:
                gr[p, dr, step - 1].wait_recv()
                if step == 2:
                    a, na = span(cnt, dr, True)
                    b, nb = span(cnt, 1 - dr, True)
                    own = tot[8 * p + a : 8 * p + a + na, rows, :].astype(F32)
                    own = own + gr_recv[p, dr, 0, a : a + na].astype(F32)
                    gr_send[p, dr, 0, a : a + na] = own.astype(BF16)
                    gr_send[p, dr, 0, b : b + nb] = tot[8 * p + b : 8 * p + b + nb, rows, :]
                else:
                    own = tot[8 * p : 8 * p + cnt, rows, :].astype(F32)
                    own = own + gr_recv[p, dr, step - 2, :cnt].astype(F32)
                    gr_send[p, dr, step - 2, :cnt] = own.astype(BF16)
                src = gr_send.at[p, dr, step - 2, pl.ds(0, cnt)]
            dst = gr_recv.at[p, dr, step - 1, pl.ds(lo, n)]
            gr[p, dr, step] = remote(
                src, dst, gr_ssem.at[p, dr, step - 1], gr_rsem.at[p, dr, step - 1], peer
            )

    for p in range(PARTS):
        for unit in ((0, 1), (2,), (), (3,))[p]:
            fd[unit, 0, far].wait_recv()
            fd[unit, 1, far].wait_recv()
        for h in range(groups[p][0], groups[p][1]):
            back(h)
        grad_step(p, 1)

    outs = []
    for k, (src, dst) in enumerate(((dk, dk_out), (dv, dv_out))):
        cp = remote(
            src.at[tokens : 2 * tokens], dst.at[:, own_cols], o_ssem.at[k], o_rsem.at[k], partner
        )
        lc = pltpu.make_async_copy(src.at[0:tokens], dst.at[:, own_cols], o_sem.at[k])
        lc.start()
        outs.append((cp, lc))

    for step in range(2, far + 1):
        for p in range(PARTS):
            grad_step(p, step)
    send_rows, finish_rows = dp_phase(n_dp, z, c, me, grad_out, *dp_refs)
    for p in range(PARTS):
        cnt = counts[p]
        own = tot[8 * p : 8 * p + cnt, rows_of(0), :].astype(F32)
        for dr in range(2):
            gr[p, dr, far].wait_recv()
            own = own + gr_recv[p, dr, far - 1, :cnt].astype(F32)
        part[0, 8 * p : 8 * p + cnt] = own[:, :8]
        part[1, 8 * p : 8 * p + cnt] = own[:, 8:]
        if cnt < 8:
            part[:, 8 * p + cnt : 8 * p + 8] = jnp.zeros((2, 8 - cnt, 8, F), F32)
        send_rows(p)
    finish_rows()

    for cp in sends:
        cp.wait_send()
    for cp, lc in outs:
        cp.wait_recv()
        lc.wait()


def dp_phase(n, z, c, me, out, part, land, fin, s1, r1, s2, r2):
    per = 32 // n
    other = 1 - c

    def rows_to(j, r):
        return pltpu.make_async_remote_copy(
            src_ref=part.at[r, pl.ds(per * j, per)], dst_ref=land.at[me, c],
            send_sem=s1.at[j, r], recv_sem=r1.at[me, c],
            device_id={"dp": j, "ctx": 2 * z + r}, device_id_type=MESH,
        )

    def rows_from(j, core):
        return pltpu.make_async_remote_copy(
            src_ref=part.at[0, pl.ds(0, per)], dst_ref=land.at[j, core],
            send_sem=s1.at[j, core], recv_sem=r1.at[j, core],
            device_id={"dp": j, "ctx": 2 * z + core}, device_id_type=MESH,
        )

    def spread(k):
        j = lax.rem(me + k, n)
        mine = fin.at[pl.ds(per * me, per)]
        return pltpu.make_async_remote_copy(
            src_ref=mine, dst_ref=mine, send_sem=s2.at[k], recv_sem=r2.at[k],
            device_id={"dp": j}, device_id_type=MESH,
        )

    def send_rows(p):
        for j in range(8 * p // per, 8 * (p + 1) // per):
            for r in range(2):

                @pl.when(2 * me + c != 2 * j + r)
                def _():
                    rows_to(j, r).start()

    def finish_rows():
        rows_from(me, other).wait_recv()
        own = part[c, pl.ds(per * me, per)]
        across = land[me, other]
        first = jnp.where(c == 0, own, across)
        second = jnp.where(c == 0, across, own)

        def take(k, carry):
            j = lax.rem(me + k, n)
            rows_from(j, 0).wait_recv()
            rows_from(j, 1).wait_recv()
            return carry[0] + land[j, 0], carry[1] + land[j, 1]

        first, second = lax.fori_loop(1, n, take, (first, second))
        both = jnp.concatenate([first, second], axis=1) / n
        fin[pl.ds(per * me, per)] = both.astype(BF16)

        def start2(k, carry):
            spread(k).start()
            return carry

        def wait2(k, carry):
            spread(k).wait_recv()
            return carry

        lax.fori_loop(1, n, start2, 0)
        lax.fori_loop(1, n, wait2, 0)
        for h in range(HH):
            for comp in range(3):
                rows = fin[3 * h + comp].astype(F32)
                out[comp, h] = rows[:8]
                out[comp, HH + h] = rows[8:]

        def wait_sent(k, carry):
            j = lax.rem(me + k, n)
            rows_from(j, 0).wait_send()
            rows_from(j, 1).wait_send()
            spread(k).wait_send()
            return carry

        rows_from(me, other).wait_send()
        lax.fori_loop(1, n, wait_sent, 0)

    return send_rows, finish_rows


def land_kernel(dk, dv, gs, dk_out, dv_out, gs_out, b0, b1, b2, in_sems, out_sems):
    trips = ((gs, b2, gs_out), (dk, b0, dk_out), (dv, b1, dv_out))
    loads = [pltpu.make_async_copy(t[0], t[1], in_sems.at[i]) for i, t in enumerate(trips)]
    stores = [pltpu.make_async_copy(t[1], t[2], out_sems.at[i]) for i, t in enumerate(trips)]
    for cp in loads:
        cp.start()
    for load, store in zip(loads, stores):
        load.wait()
        store.start()
    for cp in stores:
        cp.wait()


def dp_scratch(n_dp):
    dma = pltpu.SemaphoreType.DMA
    per = 32 // n_dp
    return [
        pltpu.VMEM((2, 32, 8, F), F32),
        pltpu.VMEM((n_dp, 2, per, 8, F), F32),
        pltpu.VMEM((32, 16, F), BF16),
        dma((n_dp, 2)),
        dma((n_dp, 2)),
        dma((n_dp,)),
        dma((n_dp,)),
    ]


def run(n_dp, n_ctx, keys_a, values_a, queries_b, grad_out, state_start, state_next):
    tokens = keys_a.shape[1]
    nz = n_ctx // 2
    far = nz // 2
    anyspace = pl.BlockSpec(memory_space=pl.ANY)
    vm = pl.BlockSpec(memory_space=pltpu.VMEM)
    flat = (tokens, H * D)
    dma = pltpu.SemaphoreType.DMA
    rows2 = 2 * tokens
    half = HH * D
    token_buf = pltpu.VMEM((rows2, half), BF16)
    mats = pltpu.VMEM((32, D, F), BF16)
    grad_shape = jax.ShapeDtypeStruct((3, H, 8, F), F32)
    dp_list = dp_scratch(n_dp)
    ring_sems = [dma((PARTS, 2, far)), dma((PARTS, 2, far))]
    outs = pl.pallas_call(
        functools.partial(main_kernel, nz, n_dp // NX, n_dp),
        out_shape=(
            jax.ShapeDtypeStruct(flat, BF16),
            jax.ShapeDtypeStruct(flat, BF16),
            grad_shape,
        ),
        in_specs=[pl.BlockSpec(memory_space=pltpu.HBM)] * 6,
        out_specs=(OUT_SPACE, OUT_SPACE, vm),
        scratch_shapes=dp_list
        + [
            token_buf, token_buf, token_buf, token_buf,
            pltpu.VMEM((2, 2, 3, HH + 1, 8, F), F32),
            mats, mats, mats, mats,
            pltpu.VMEM((3 * HH, D, F), F32),
            pltpu.VMEM((2, PARTS, 2, far - 1, D, F), BF16),
            pltpu.VMEM((2, PARTS, 2, far, D, F), BF16),
            mats,
            pltpu.VMEM((HH, 3, rows2, F), F32),
            pltpu.VMEM((HH, 3, rows2, F), F32),
            pltpu.VMEM((HH, 3, rows2, F), BF16),
            token_buf, token_buf,
            mats,
            pltpu.VMEM((PARTS, 2, far - 1, 8, 16, F), BF16),
            pltpu.VMEM((PARTS, 2, far, 8, 16, F), BF16),
            dma((6,)), dma((6,)), dma((6,)),
            dma((2, far)), dma((2, far)),
            dma((2, 2, 2)), dma((2, 2, 2)),
        ]
        + ring_sems
        + [dma((2, PARTS, 2, far)), dma((2, PARTS, 2, far))]
        + ring_sems
        + ring_sems
        + [dma((2,)), dma((2,)), dma((2,))],
        compiler_params=pltpu.CompilerParams(
            collective_id=0, has_side_effects=True, vmem_limit_bytes=RING_VMEM
        ),
        name="ttt_ring",
    )(
        keys_a.reshape(flat),
        values_a.reshape(flat),
        queries_b.reshape(flat),
        grad_out.reshape(flat),
        state_start,
        state_next[0],
    )
    dk, dv, gs = pl.pallas_call(
        land_kernel,
        out_shape=(
            jax.ShapeDtypeStruct(flat, BF16),
            jax.ShapeDtypeStruct(flat, BF16),
            grad_shape,
        ),
        in_specs=[LAND_SPACE] * 3,
        out_specs=(anyspace,) * 3,
        scratch_shapes=[
            pltpu.VMEM(flat, BF16), pltpu.VMEM(flat, BF16), pltpu.VMEM((3, H, 8, F), F32),
            dma((3,)), dma((3,)),
        ],
        compiler_params=pltpu.CompilerParams(vmem_limit_bytes=LAND_VMEM),
        name="land",
    )(*outs)
    return dk.reshape(keys_a.shape), dv.reshape(keys_a.shape), gs


OUT_SPACE = pl.BlockSpec(memory_space=pl.ANY)
LAND_SPACE = pl.BlockSpec(memory_space=pltpu.HBM)
RING_VMEM = 56 * 1024 * 1024
LAND_VMEM = 56 * 1024 * 1024


def solution(mesh):
    placed = (
        P("dp", "ctx", None),
        P("dp", "ctx", None),
        P("dp", "ctx", None),
        P("dp", "ctx", None),
        P(None, None, "ctx", None),
        P("dp", None, None, "ctx", None),
    )
    return jax.shard_map(
        functools.partial(run, mesh.shape["dp"], mesh.shape["ctx"]),
        mesh=mesh,
        in_specs=placed,
        out_specs=(P("dp", "ctx", None), P("dp", "ctx", None), P(None, None, "ctx", None)),
        check_vma=False,
    )
```

```python
import functools

import jax
import jax.numpy as jnp
from jax import lax
from jax.experimental import pallas as pl
from jax.experimental.pallas import tpu as pltpu
from jax.sharding import PartitionSpec as P

D = 128
H = 20
F = 128
HH = H // 2
RATE = 4.0
CA = 3.4445
CB = -4.775
CC = 2.0315
MESH = pl.DeviceIdType.MESH
F32 = jnp.float32
BF16 = jnp.bfloat16


def mm(a, b):
    return jnp.dot(a, b, preferred_element_type=F32)


def mm_tn(a, b):
    return lax.dot_general(a, b, (((0,), (0,)), ((), ())), preferred_element_type=F32)


def mm_nt(a, b):
    return lax.dot_general(a, b, (((1,), (1,)), ((), ())), preferred_element_type=F32)


def newton_forward(mats):
    norms, units, xs, grams, polys = [], [], [], [], []
    for g in mats:
        total = jnp.sum(jnp.sum(g * g, axis=1, keepdims=True), axis=0, keepdims=True)
        n = jnp.sqrt(total + 1e-06)
        u = g / n
        norms.append(n)
        units.append(u)
    x = [u.astype(BF16) for u in units]
    for step in range(2):
        a = [mm_nt(v, v).astype(BF16) for v in x]
        sq = [mm(v, v) for v in a]
        p = [(CB * v.astype(F32) + CC * w).astype(BF16) for v, w in zip(a, sq)]
        xs.append(x)
        grams.append(a)
        polys.append(p)
        if step == 0:
            mixed = [mm(v, w) for v, w in zip(p, x)]
            x = [(CA * v.astype(F32) + w).astype(BF16) for v, w in zip(x, mixed)]
    return norms, units, xs, grams, polys


def newton_backward(saved, cts):
    norms, units, xs, grams, polys = saved
    ct = cts
    for step in (1, 0):
        x, a, p = xs[step], grams[step], polys[step]
        ct_z = [mm_nt(v, w).astype(BF16) for v, w in zip(ct, x)]
        direct = [CA * v.astype(F32) + mm(w, v) for v, w in zip(ct, p)]
        ct_a = [
            (CB * v.astype(F32) + CC * (mm(v, w) + mm(w, v))).astype(BF16)
            for v, w in zip(ct_z, a)
        ]
        ct = [
            (d + mm(v, w) + mm_tn(v, w)).astype(BF16) for d, v, w in zip(direct, ct_a, x)
        ]
    out = []
    for n, u, v in zip(norms, units, ct):
        v = v.astype(F32)
        dot = jnp.sum(jnp.sum(v * u, axis=1, keepdims=True), axis=0, keepdims=True)
        out.append((v - u * dot) / n)
    return out


NX = 4
PARTS = 4


def main_kernel(
    nz, ny, n_dp,
    keys, values, queries, gout, start, nxt,
    *refs,
):
    dk_out, dv_out, grad_out = refs[:3]
    dp_refs, refs = refs[3:10], refs[10:]
    part = dp_refs[0]
    (
        xk, xv, xq, xo, stage, ws, wn, gbuf, sbuf, psum,
        rs_send, rs_recv, field, act, aux, rnd, dk, dv, tot, gr_send, gr_recv,
        in_sem, x_ssem, x_rsem, st_ssem, st_rsem, sx_ssem, sx_rsem, ag_ssem, ag_rsem,
        rs_ssem, rs_rsem, f_ssem, f_rsem, gr_ssem, gr_rsem, o_sem, o_ssem, o_rsem, word,
    ) = refs
    ctx = lax.axis_index("ctx")
    z = lax.div(ctx, 2)
    c = lax.rem(ctx, 2)
    other = 1 - c
    me = lax.axis_index("dp")
    xi = lax.div(me, ny)
    yi = lax.rem(me, ny)

    def chip(offset):
        return lax.rem(z + offset + 2 * nz, nz)

    def xpos(offset):
        return lax.rem(xi + offset + 2 * NX, NX)

    right = {"ctx": 2 * chip(1) + c}
    left = {"ctx": 2 * chip(-1) + c}
    partner = {"ctx": 2 * z + other}
    xright = {"dp": xpos(1) * ny + yi}
    xleft = {"dp": xpos(-1) * ny + yi}
    half = HH * D
    dirs = ((right, 1), (left, -1))
    xdirs = ((xright, 1), (xleft, -1))
    far = nz // 2

    own_heads = pl.ds(c * HH, HH)
    other_heads = pl.ds(other * HH, HH)
    own_cols = pl.ds(pl.multiple_of(c * half, 128), half)
    other_cols = pl.ds(pl.multiple_of(other * half, 128), half)
    tokens = keys.shape[0]

    locals_in = []
    for k, st in enumerate((start, nxt)):
        lc = pltpu.make_async_copy(
            st.at[:, own_heads], stage.at[k, c, :, pl.ds(0, HH)], in_sem.at[k]
        )
        lc.start()
        locals_in.append(lc)
    token_pairs = ((queries, xq), (gout, xo), (keys, xk), (values, xv))
    for k, (src, dst) in enumerate(token_pairs):
        lc = pltpu.make_async_copy(src.at[:, own_cols], dst.at[0:tokens], in_sem.at[2 + k])
        lc.start()
        locals_in.append(lc)

    barrier = pltpu.get_barrier_semaphore()
    around = [partner, xright, xleft]
    if ny > 1:
        around.append({"dp": xi * ny + lax.rem(yi + 1, ny)})
        around.append({"dp": xi * ny + lax.rem(yi + ny - 1, ny)})
    near = [right, left] + around
    for peer in near:
        pl.semaphore_signal(barrier, inc=1, device_id=peer, device_id_type=MESH)
    pl.semaphore_wait(barrier, len(near))

    def pass_word(step):
        for peer in around:
            pl.semaphore_signal(word.at[step], inc=1, device_id=peer, device_id_type=MESH)
        pl.semaphore_wait(word.at[step], len(around))

    sends = []

    def remote(src, dst, ssem, rsem, peer):
        cp = pltpu.make_async_remote_copy(
            src_ref=src, dst_ref=dst, send_sem=ssem, recv_sem=rsem,
            device_id=peer, device_id_type=MESH,
        )
        cp.start()
        sends.append(cp)
        return cp

    remotes_in = []
    for k, st in enumerate((start, nxt)):
        remotes_in.append(
            remote(
                st.at[:, other_heads], stage.at[k, c, :, pl.ds(0, HH)],
                x_ssem.at[k], x_rsem.at[k], partner,
            )
        )

    def swap_tokens(k):
        src, dst = token_pairs[k]
        remotes_in.append(
            remote(
                src.at[:, other_cols], dst.at[tokens : 2 * tokens],
                x_ssem.at[2 + k], x_rsem.at[2 + k], partner,
            )
        )

    def rows_of(offset):
        return pl.ds(pl.multiple_of(16 * chip(offset), 16), 16)

    for cc in range(2):
        for comp in range(3):
            stage[0, cc, comp, HH] = jnp.zeros((8, F), F32)
    locals_in[0].wait()
    remotes_in[0].wait_recv()
    quarter = pl.multiple_of(8 * xi, 8)
    for i in range(8):
        m = quarter + i
        h, comp = lax.div(m, 3), lax.rem(m, 3)
        ws[m, rows_of(0), :] = jnp.concatenate(
            [stage[0, 0, comp, h], stage[0, 1, comp, h]], axis=0
        ).astype(BF16)

    counts = [8, 8, 8, 3 * HH - 24]

    def span(cnt, dr, last):
        if not last:
            return 0, cnt
        return (0, cnt // 2) if dr == 0 else (cnt // 2, cnt - cnt // 2)

    ag = {}

    def gather_step(unit, step):
        for dr, (peer, sign) in enumerate(dirs):
            if step > 1:
                ag[unit, dr, step - 1].wait_recv()
            if unit == 0:
                ref, base, cnt = ws, quarter, 8
                sems = st_ssem.at[dr, step - 1], st_rsem.at[dr, step - 1]
            else:
                ref, base, cnt = wn, 8 * (unit - 1), counts[unit - 1]
                sems = ag_ssem.at[unit - 1, dr, step - 1], ag_rsem.at[unit - 1, dr, step - 1]
            lo, n = span(cnt, dr, step == far)
            piece = ref.at[pl.ds(base + lo, n), rows_of(-sign * (step - 1)), :]
            ag[unit, dr, step] = remote(piece, piece, sems[0], sems[1], peer)

    gather_step(0, 1)
    locals_in[1].wait()
    remotes_in[1].wait_recv()
    for p in range(PARTS):
        for i in range(counts[p]):
            m = 8 * p + i
            h, comp = m // 3, m % 3
            wn[m, rows_of(0), :] = jnp.concatenate(
                [stage[1, 0, comp, h], stage[1, 1, comp, h]], axis=0
            ).astype(BF16)
        gather_step(1 + p, 1)
    for step in range(2, far + 1):
        for unit in range(1 + PARTS):
            gather_step(unit, step)
        if step == 2:
            swap_tokens(0)
            swap_tokens(1)
        if step == far:
            swap_tokens(2)
            swap_tokens(3)

    sx = {}

    def xgather(i, step):
        for dr, (peer, sign) in enumerate(xdirs):
            lo, n = 4 * i, 4
            if step == 2:
                sx[i, dr, 1].wait_recv()
                lo, n = (4 * i, 2) if dr == 0 else (4 * i + 2, 2)
            base = pl.multiple_of(8 * xpos(-sign * (step - 1)), 8)
            piece = ws.at[pl.ds(base + lo, n)]
            sx[i, dr, step] = remote(
                piece, piece, sx_ssem.at[i, dr, step - 1], sx_rsem.at[i, dr, step - 1], peer
            )

    ag[0, 0, far].wait_recv()
    ag[0, 1, far].wait_recv()
    xgather(0, 1)
    xgather(1, 1)
    pass_word(0)

    def phi(h, xs, ys, w):
        cols = slice(h * D, (h + 1) * D)
        x, y = xs[:, cols], ys[:, cols]
        gu = mm(x, jnp.concatenate([w[3 * h], w[3 * h + 1]], axis=1))
        proj = mm(y, w[3 * h + 2])
        gate, up = gu[:, :F], gu[:, F:]
        s = jax.nn.sigmoid(gate)
        swish = gate * s
        hidden = (swish * up).astype(BF16)
        d_gate = (proj * up * s * (1.0 + gate * (1.0 - s))).astype(BF16)
        d_up = (proj * swish).astype(BF16)
        gab = mm_tn(x, jnp.concatenate([d_gate, d_up], axis=1))
        gc = mm_tn(y, hidden)
        return gate, up, proj, hidden, d_gate, d_up, (gab[:, :F], gab[:, F:], gc)

    def phi_a(h):
        gate, up, proj, hidden, d_gate, d_up, grads = phi(h, xk, xv, ws)
        act[h, 0] = gate
        act[h, 1] = up
        act[h, 2] = proj
        rnd[h, 0] = d_gate
        rnd[h, 1] = d_up
        rnd[h, 2] = hidden
        for i in range(3):
            gbuf[3 * h + i] = grads[i].astype(BF16)

    def phi_b(h):
        grads = phi(h, xq, xo, wn)[-1]
        for i in range(3):
            psum[3 * h + i] = grads[i]
            sbuf[3 * h + i] = grads[i].astype(BF16)

    for pad in (3 * HH, 3 * HH + 1):
        gbuf[pad] = jnp.zeros((D, F), BF16)
        sbuf[pad] = jnp.zeros((D, F), BF16)

    bufs = (gbuf, sbuf)
    rs = {}
    rows_half = D // 2

    def rs_step(k, p, step):
        for dr, (peer, sign) in enumerate(dirs):
            slot = 8 * p + chip(sign * (far + 1 - step))
            lo, n = (0, D)
            if step == 1:
                lo, n = (0, rows_half) if dr == 0 else (rows_half, rows_half)
                src = bufs[k].at[slot, pl.ds(lo, n)]
            else:
                rs[k, p, dr, step - 1].wait_recv()
                if step == 2:
                    a = 0 if dr == 0 else rows_half
                    b = rows_half - a
                    part_sum = bufs[k][slot, a : a + rows_half].astype(F32) + rs_recv[
                        k, p, dr, 0, a : a + rows_half
                    ].astype(F32)
                    rs_send[k, p, dr, 0, a : a + rows_half] = part_sum.astype(BF16)
                    rs_send[k, p, dr, 0, b : b + rows_half] = bufs[k][slot, b : b + rows_half]
                else:
                    total = bufs[k][slot].astype(F32) + rs_recv[k, p, dr, step - 2].astype(F32)
                    rs_send[k, p, dr, step - 2] = total.astype(BF16)
                src = rs_send.at[k, p, dr, step - 2]
            dst = rs_recv.at[k, p, dr, step - 1, pl.ds(lo, n)]
            rs[k, p, dr, step] = remote(
                src, dst, rs_ssem.at[k, p, dr, step - 1], rs_rsem.at[k, p, dr, step - 1], peer
            )

    def rs_total(k, parts):
        out = []
        for p in parts:
            v = bufs[k][8 * p + z].astype(F32)
            for dr in range(2):
                rs[k, p, dr, far].wait_recv()
                v = v + rs_recv[k, p, dr, far - 1].astype(F32)
            out.append(v)
        return out

    groups = ((0, 3), (3, 6), (6, 8), (8, HH))
    for k in range(2):
        locals_in[2 + k].wait()
        remotes_in[2 + k].wait_recv()
    for p in range(PARTS):
        for unit in ((1, 2), (3,), (), (4,))[p]:
            ag[unit, 0, far].wait_recv()
            ag[unit, 1, far].wait_recv()
        for h in range(groups[p][0], groups[p][1]):
            phi_b(h)
        rs_step(1, p, 1)
    pass_word(1)
    xgather(0, 2)
    for p in range(PARTS):
        rs_step(1, p, 2)
    xgather(1, 2)
    pass_word(2)
    for step in range(3, far + 1):
        for p in range(PARTS):
            rs_step(1, p, step)
    for i in range(2):
        sx[i, 0, 2].wait_recv()
        sx[i, 1, 2].wait_recv()
    for k in range(2):
        locals_in[4 + k].wait()
        remotes_in[4 + k].wait_recv()
    for p in range(PARTS):
        for h in range(groups[p][0], groups[p][1]):
            phi_a(h)
        rs_step(0, p, 1)
    pass_word(3)
    cts = [(RATE * v).astype(BF16) for v in rs_total(1, range(PARTS))]
    for step in range(2, far + 1):
        for p in range(PARTS):
            rs_step(0, p, step)
    fd = {}

    def field_step(p, step):
        for dr, (peer, sign) in enumerate(dirs):
            if step > 1:
                fd[p, dr, step - 1].wait_recv()
            lo, n = span(D, dr, step == far)
            piece = field.at[8 * p + chip(-sign * (step - 1)), pl.ds(lo, n)]
            fd[p, dr, step] = remote(
                piece, piece, f_ssem.at[p, dr, step - 1], f_rsem.at[p, dr, step - 1], peer
            )

    pass_word(4)
    for pair in ((0, 1), (2, 3)):
        saved = newton_forward(rs_total(0, pair))
        fields = newton_backward(saved, [cts[p] for p in pair])
        for p, value in zip(pair, fields):
            field[8 * p + z] = value.astype(BF16)
            field_step(p, 1)

    def ready(h):
        gate, up, proj = act[h, 0], act[h, 1], act[h, 2]
        s = jax.nn.sigmoid(gate)
        sd = s * (1.0 - s)
        aux[h, 0] = gate * s
        aux[h, 1] = s + gate * sd
        aux[h, 2] = (proj * up) * (sd * (2.0 + gate * (1.0 - 2.0 * s)))

    for step in range(2, far + 1):
        for h in range(HH * (step - 2) // (far - 1), HH * (step - 1) // (far - 1)):
            ready(h)
        for p in range(PARTS):
            field_step(p, step)

    def back(h):
        cols = slice(h * D, (h + 1) * D)
        x, y = xk[:, cols], xv[:, cols]
        up, proj = act[h, 1], act[h, 2]
        swish, q, bend = aux[h, 0], aux[h, 1], aux[h, 2]
        d_gate, d_up, hidden = rnd[h, 0], rnd[h, 1], rnd[h, 2]
        da, db, dc = field[3 * h], field[3 * h + 1], field[3 * h + 2]
        dab = jnp.concatenate([da, db], axis=1)
        ct_gu = mm(x, dab).astype(BF16).astype(F32)
        ct_dg, ct_du = ct_gu[:, :F], ct_gu[:, F:]
        ct_h = mm(y, dc).astype(BF16).astype(F32)
        ct_w = ct_h * up + ct_du * proj
        cq = ct_dg * q
        ct_up = (ct_h * swish + cq * proj).astype(BF16)
        ct_p = (ct_du * swish + cq * up).astype(BF16)
        ct_gate = (ct_w * q + ct_dg * bend).astype(BF16)
        wab = jnp.concatenate([ws[3 * h], ws[3 * h + 1]], axis=1)
        ct_ab = jnp.concatenate([ct_gate, ct_up], axis=1)
        d_ab = jnp.concatenate([d_gate, d_up], axis=1)
        dx = mm_nt(d_ab, dab) + mm_nt(ct_ab, wab)
        dy = mm_nt(hidden, dc) + mm_nt(ct_p, ws[3 * h + 2])
        dk[:, cols] = dx.astype(BF16)
        dv[:, cols] = dy.astype(BF16)
        wg = mm_tn(x, ct_ab)
        tot[3 * h] = (psum[3 * h] + wg[:, :F]).astype(BF16)
        tot[3 * h + 1] = (psum[3 * h + 1] + wg[:, F:]).astype(BF16)
        tot[3 * h + 2] = (psum[3 * h + 2] + mm_tn(y, ct_p)).astype(BF16)

    pass_word(5)

    gr = {}

    def grad_step(p, step):
        cnt = counts[p]
        for dr, (peer, sign) in enumerate(dirs):
            rows = rows_of(sign * (far + 1 - step))
            lo, n = span(cnt, dr, step == 1)
            if step == 1:
                src = tot.at[pl.ds(8 * p + lo, n), rows, :]
            else:
                gr[p, dr, step - 1].wait_recv()
                if step == 2:
                    a, na = span(cnt, dr, True)
                    b, nb = span(cnt, 1 - dr, True)
                    own = tot[8 * p + a : 8 * p + a + na, rows, :].astype(F32)
                    own = own + gr_recv[p, dr, 0, a : a + na].astype(F32)
                    gr_send[p, dr, 0, a : a + na] = own.astype(BF16)
                    gr_send[p, dr, 0, b : b + nb] = tot[8 * p + b : 8 * p + b + nb, rows, :]
                else:
                    own = tot[8 * p : 8 * p + cnt, rows, :].astype(F32)
                    own = own + gr_recv[p, dr, step - 2, :cnt].astype(F32)
                    gr_send[p, dr, step - 2, :cnt] = own.astype(BF16)
                src = gr_send.at[p, dr, step - 2, pl.ds(0, cnt)]
            dst = gr_recv.at[p, dr, step - 1, pl.ds(lo, n)]
            gr[p, dr, step] = remote(
                src, dst, gr_ssem.at[p, dr, step - 1], gr_rsem.at[p, dr, step - 1], peer
            )

    for p in range(PARTS):
        for unit in ((0, 1), (2,), (), (3,))[p]:
            fd[unit, 0, far].wait_recv()
            fd[unit, 1, far].wait_recv()
        for h in range(groups[p][0], groups[p][1]):
            back(h)
        grad_step(p, 1)

    for step in range(2, far + 1):
        for p in range(PARTS):
            grad_step(p, step)
        if step == far - 1:
            outs = []
            for k, (src, dst) in enumerate(((dk, dk_out), (dv, dv_out))):
                cp = remote(
                    src.at[tokens : 2 * tokens], dst.at[:, own_cols], o_ssem.at[k], o_rsem.at[k], partner
                )
                lc = pltpu.make_async_copy(src.at[0:tokens], dst.at[:, own_cols], o_sem.at[k])
                lc.start()
                outs.append((cp, lc))
    send_rows, finish_rows = dp_phase(n_dp, z, c, me, grad_out, *dp_refs)
    for p in range(PARTS):
        cnt = counts[p]
        own = tot[8 * p : 8 * p + cnt, rows_of(0), :].astype(F32)
        for dr in range(2):
            gr[p, dr, far].wait_recv()
            own = own + gr_recv[p, dr, far - 1, :cnt].astype(F32)
        part[0, 8 * p : 8 * p + cnt] = own[:, :8]
        part[1, 8 * p : 8 * p + cnt] = own[:, 8:]
        if cnt < 8:
            part[:, 8 * p + cnt : 8 * p + 8] = jnp.zeros((2, 8 - cnt, 8, F), F32)
        send_rows(p)
    finish_rows()

    for cp in sends:
        cp.wait_send()
    for cp, lc in outs:
        cp.wait_recv()
        lc.wait()


def dp_phase(n, z, c, me, out, part, land, fin, s1, r1, s2, r2):
    per = 32 // n
    other = 1 - c

    def rows_to(j, r):
        return pltpu.make_async_remote_copy(
            src_ref=part.at[r, pl.ds(per * j, per)], dst_ref=land.at[me, c],
            send_sem=s1.at[j, r], recv_sem=r1.at[me, c],
            device_id={"dp": j, "ctx": 2 * z + r}, device_id_type=MESH,
        )

    def rows_from(j, core):
        return pltpu.make_async_remote_copy(
            src_ref=part.at[0, pl.ds(0, per)], dst_ref=land.at[j, core],
            send_sem=s1.at[j, core], recv_sem=r1.at[j, core],
            device_id={"dp": j, "ctx": 2 * z + core}, device_id_type=MESH,
        )

    def spread(k):
        j = lax.rem(me + k, n)
        mine = fin.at[pl.ds(per * me, per)]
        return pltpu.make_async_remote_copy(
            src_ref=mine, dst_ref=mine, send_sem=s2.at[k], recv_sem=r2.at[k],
            device_id={"dp": j}, device_id_type=MESH,
        )

    def send_rows(p):
        for j in range(8 * p // per, 8 * (p + 1) // per):
            for r in range(2):

                @pl.when(2 * me + c != 2 * j + r)
                def _():
                    rows_to(j, r).start()

    def finish_rows():
        rows_from(me, other).wait_recv()
        own = part[c, pl.ds(per * me, per)]
        across = land[me, other]
        first = jnp.where(c == 0, own, across)
        second = jnp.where(c == 0, across, own)

        def take(k, carry):
            j = lax.rem(me + k, n)
            rows_from(j, 0).wait_recv()
            rows_from(j, 1).wait_recv()
            return carry[0] + land[j, 0], carry[1] + land[j, 1]

        first, second = lax.fori_loop(1, n, take, (first, second))
        both = jnp.concatenate([first, second], axis=1) / n
        fin[pl.ds(per * me, per)] = both.astype(BF16)

        def start2(k, carry):
            spread(k).start()
            return carry

        def wait2(k, carry):
            spread(k).wait_recv()
            return carry

        lax.fori_loop(1, n, start2, 0)
        lax.fori_loop(1, n, wait2, 0)
        for h in range(HH):
            for comp in range(3):
                rows = fin[3 * h + comp].astype(F32)
                out[comp, h] = rows[:8]
                out[comp, HH + h] = rows[8:]

        def wait_sent(k, carry):
            j = lax.rem(me + k, n)
            rows_from(j, 0).wait_send()
            rows_from(j, 1).wait_send()
            spread(k).wait_send()
            return carry

        rows_from(me, other).wait_send()
        lax.fori_loop(1, n, wait_sent, 0)

    return send_rows, finish_rows


def land_kernel(dk, dv, gs, dk_out, dv_out, gs_out, b0, b1, b2, in_sems, out_sems):
    trips = ((gs, b2, gs_out), (dk, b0, dk_out), (dv, b1, dv_out))
    loads = [pltpu.make_async_copy(t[0], t[1], in_sems.at[i]) for i, t in enumerate(trips)]
    stores = [pltpu.make_async_copy(t[1], t[2], out_sems.at[i]) for i, t in enumerate(trips)]
    for cp in loads:
        cp.start()
    for load, store in zip(loads, stores):
        load.wait()
        store.start()
    for cp in stores:
        cp.wait()


def dp_scratch(n_dp):
    dma = pltpu.SemaphoreType.DMA
    per = 32 // n_dp
    return [
        pltpu.VMEM((2, 32, 8, F), F32),
        pltpu.VMEM((n_dp, 2, per, 8, F), F32),
        pltpu.VMEM((32, 16, F), BF16),
        dma((n_dp, 2)),
        dma((n_dp, 2)),
        dma((n_dp,)),
        dma((n_dp,)),
    ]


def run(n_dp, n_ctx, keys_a, values_a, queries_b, grad_out, state_start, state_next):
    tokens = keys_a.shape[1]
    nz = n_ctx // 2
    far = nz // 2
    anyspace = pl.BlockSpec(memory_space=pl.ANY)
    vm = pl.BlockSpec(memory_space=pltpu.VMEM)
    flat = (tokens, H * D)
    dma = pltpu.SemaphoreType.DMA
    rows2 = 2 * tokens
    half = HH * D
    token_buf = pltpu.VMEM((rows2, half), BF16)
    mats = pltpu.VMEM((32, D, F), BF16)
    grad_shape = jax.ShapeDtypeStruct((3, H, 8, F), F32)
    dp_list = dp_scratch(n_dp)
    ring_sems = [dma((PARTS, 2, far)), dma((PARTS, 2, far))]
    outs = pl.pallas_call(
        functools.partial(main_kernel, nz, n_dp // NX, n_dp),
        out_shape=(
            jax.ShapeDtypeStruct(flat, BF16),
            jax.ShapeDtypeStruct(flat, BF16),
            grad_shape,
        ),
        in_specs=[pl.BlockSpec(memory_space=pltpu.HBM)] * 6,
        out_specs=(OUT_SPACE, OUT_SPACE, vm),
        scratch_shapes=dp_list
        + [
            token_buf, token_buf, token_buf, token_buf,
            pltpu.VMEM((2, 2, 3, HH + 1, 8, F), F32),
            mats, mats, mats, mats,
            pltpu.VMEM((3 * HH, D, F), F32),
            pltpu.VMEM((2, PARTS, 2, far - 1, D, F), BF16),
            pltpu.VMEM((2, PARTS, 2, far, D, F), BF16),
            mats,
            pltpu.VMEM((HH, 3, rows2, F), F32),
            pltpu.VMEM((HH, 3, rows2, F), F32),
            pltpu.VMEM((HH, 3, rows2, F), BF16),
            token_buf, token_buf,
            mats,
            pltpu.VMEM((PARTS, 2, far - 1, 8, 16, F), BF16),
            pltpu.VMEM((PARTS, 2, far, 8, 16, F), BF16),
            dma((6,)), dma((6,)), dma((6,)),
            dma((2, far)), dma((2, far)),
            dma((2, 2, 2)), dma((2, 2, 2)),
        ]
        + ring_sems
        + [dma((2, PARTS, 2, far)), dma((2, PARTS, 2, far))]
        + ring_sems
        + ring_sems
        + [dma((2,)), dma((2,)), dma((2,)), pltpu.SemaphoreType.REGULAR((NX // 2 + 4,))],
        compiler_params=pltpu.CompilerParams(
            collective_id=0, has_side_effects=True, vmem_limit_bytes=RING_VMEM
        ),
        name="ttt_ring",
    )(
        keys_a.reshape(flat),
        values_a.reshape(flat),
        queries_b.reshape(flat),
        grad_out.reshape(flat),
        state_start,
        state_next[0],
    )
    dk, dv, gs = pl.pallas_call(
        land_kernel,
        out_shape=(
            jax.ShapeDtypeStruct(flat, BF16),
            jax.ShapeDtypeStruct(flat, BF16),
            grad_shape,
        ),
        in_specs=[LAND_SPACE] * 3,
        out_specs=(anyspace,) * 3,
        scratch_shapes=[
            pltpu.VMEM(flat, BF16), pltpu.VMEM(flat, BF16), pltpu.VMEM((3, H, 8, F), F32),
            dma((3,)), dma((3,)),
        ],
        compiler_params=pltpu.CompilerParams(vmem_limit_bytes=LAND_VMEM),
        name="land",
    )(*outs)
    return dk.reshape(keys_a.shape), dv.reshape(keys_a.shape), gs


OUT_SPACE = pl.BlockSpec(memory_space=pl.ANY)
LAND_SPACE = pl.BlockSpec(memory_space=pltpu.HBM)
RING_VMEM = 56 * 1024 * 1024
LAND_VMEM = 56 * 1024 * 1024


def solution(mesh):
    placed = (
        P("dp", "ctx", None),
        P("dp", "ctx", None),
        P("dp", "ctx", None),
        P("dp", "ctx", None),
        P(None, None, "ctx", None),
        P("dp", None, None, "ctx", None),
    )
    return jax.shard_map(
        functools.partial(run, mesh.shape["dp"], mesh.shape["ctx"]),
        mesh=mesh,
        in_specs=placed,
        out_specs=(P("dp", "ctx", None), P("dp", "ctx", None), P(None, None, "ctx", None)),
        check_vma=False,
    )
```

```python
import functools

import jax
import jax.numpy as jnp
from jax import lax
from jax.experimental import pallas as pl
from jax.experimental.pallas import tpu as pltpu
from jax.sharding import PartitionSpec as P

D = 128
H = 20
F = 128
HH = H // 2
RATE = 4.0
CA = 3.4445
CB = -4.775
CC = 2.0315
MESH = pl.DeviceIdType.MESH
F32 = jnp.float32
BF16 = jnp.bfloat16


def mm(a, b):
    return jnp.dot(a, b, preferred_element_type=F32)


def mm_tn(a, b):
    return lax.dot_general(a, b, (((0,), (0,)), ((), ())), preferred_element_type=F32)


def mm_nt(a, b):
    return lax.dot_general(a, b, (((1,), (1,)), ((), ())), preferred_element_type=F32)


def newton_forward(mats):
    norms, units, xs, grams, polys = [], [], [], [], []
    for g in mats:
        total = jnp.sum(jnp.sum(g * g, axis=1, keepdims=True), axis=0, keepdims=True)
        n = jnp.sqrt(total + 1e-06)
        u = g / n
        norms.append(n)
        units.append(u)
    x = [u.astype(BF16) for u in units]
    for step in range(2):
        a = [mm_nt(v, v).astype(BF16) for v in x]
        sq = [mm(v, v) for v in a]
        p = [(CB * v.astype(F32) + CC * w).astype(BF16) for v, w in zip(a, sq)]
        xs.append(x)
        grams.append(a)
        polys.append(p)
        if step == 0:
            mixed = [mm(v, w) for v, w in zip(p, x)]
            x = [(CA * v.astype(F32) + w).astype(BF16) for v, w in zip(x, mixed)]
    return norms, units, xs, grams, polys


def newton_backward(saved, cts):
    norms, units, xs, grams, polys = saved
    ct = cts
    for step in (1, 0):
        x, a, p = xs[step], grams[step], polys[step]
        ct_z = [mm_nt(v, w).astype(BF16) for v, w in zip(ct, x)]
        direct = [CA * v.astype(F32) + mm(w, v) for v, w in zip(ct, p)]
        ct_a = [
            (CB * v.astype(F32) + CC * (mm(v, w) + mm(w, v))).astype(BF16)
            for v, w in zip(ct_z, a)
        ]
        ct = [
            (d + mm(v, w) + mm_tn(v, w)).astype(BF16) for d, v, w in zip(direct, ct_a, x)
        ]
    out = []
    for n, u, v in zip(norms, units, ct):
        v = v.astype(F32)
        dot = jnp.sum(jnp.sum(v * u, axis=1, keepdims=True), axis=0, keepdims=True)
        out.append((v - u * dot) / n)
    return out


NX = 4
PARTS = 4


def main_kernel(
    nz, ny, n_dp,
    keys, values, queries, gout, start, nxt,
    *refs,
):
    dk_out, dv_out, grad_out = refs[:3]
    dp_refs, refs = refs[3:10], refs[10:]
    part = dp_refs[0]
    (
        xk, xv, xq, xo, stage, ws, wn, gbuf, sbuf, psum,
        rs_send, rs_recv, field, act, aux, rnd, dk, dv, tot, gr_send, gr_recv,
        in_sem, x_ssem, x_rsem, st_ssem, st_rsem, sx_ssem, sx_rsem, ag_ssem, ag_rsem,
        rs_ssem, rs_rsem, f_ssem, f_rsem, gr_ssem, gr_rsem, o_sem, o_ssem, o_rsem, word,
    ) = refs
    ctx = lax.axis_index("ctx")
    z = lax.div(ctx, 2)
    c = lax.rem(ctx, 2)
    other = 1 - c
    me = lax.axis_index("dp")
    xi = lax.div(me, ny)
    yi = lax.rem(me, ny)

    def chip(offset):
        return lax.rem(z + offset + 2 * nz, nz)

    def xpos(offset):
        return lax.rem(xi + offset + 2 * NX, NX)

    right = {"ctx": 2 * chip(1) + c}
    left = {"ctx": 2 * chip(-1) + c}
    partner = {"ctx": 2 * z + other}
    xright = {"dp": xpos(1) * ny + yi}
    xleft = {"dp": xpos(-1) * ny + yi}
    half = HH * D
    dirs = ((right, 1), (left, -1))
    xdirs = ((xright, 1), (xleft, -1))
    far = nz // 2

    own_heads = pl.ds(c * HH, HH)
    other_heads = pl.ds(other * HH, HH)
    own_cols = pl.ds(pl.multiple_of(c * half, 128), half)
    other_cols = pl.ds(pl.multiple_of(other * half, 128), half)
    tokens = keys.shape[0]

    locals_in = []
    for k, st in enumerate((start, nxt)):
        lc = pltpu.make_async_copy(
            st.at[:, own_heads], stage.at[k, c, :, pl.ds(0, HH)], in_sem.at[k]
        )
        lc.start()
        locals_in.append(lc)
    token_pairs = ((queries, xq), (gout, xo), (keys, xk), (values, xv))
    for k, (src, dst) in enumerate(token_pairs):
        lc = pltpu.make_async_copy(src.at[:, own_cols], dst.at[0:tokens], in_sem.at[2 + k])
        lc.start()
        locals_in.append(lc)

    barrier = pltpu.get_barrier_semaphore()
    around = [partner, xright, xleft]
    if ny > 1:
        around.append({"dp": xi * ny + lax.rem(yi + 1, ny)})
        around.append({"dp": xi * ny + lax.rem(yi + ny - 1, ny)})
    near = [right, left] + around
    for peer in near:
        pl.semaphore_signal(barrier, inc=1, device_id=peer, device_id_type=MESH)
    pl.semaphore_wait(barrier, len(near))

    def pass_word(step):
        for peer in around:
            pl.semaphore_signal(word.at[step], inc=1, device_id=peer, device_id_type=MESH)
        pl.semaphore_wait(word.at[step], len(around))

    sends = []

    def remote(src, dst, ssem, rsem, peer):
        cp = pltpu.make_async_remote_copy(
            src_ref=src, dst_ref=dst, send_sem=ssem, recv_sem=rsem,
            device_id=peer, device_id_type=MESH,
        )
        cp.start()
        sends.append(cp)
        return cp

    remotes_in = []
    for k, st in enumerate((start, nxt)):
        remotes_in.append(
            remote(
                st.at[:, other_heads], stage.at[k, c, :, pl.ds(0, HH)],
                x_ssem.at[k], x_rsem.at[k], partner,
            )
        )

    def swap_tokens(k):
        src, dst = token_pairs[k]
        remotes_in.append(
            remote(
                src.at[:, other_cols], dst.at[tokens : 2 * tokens],
                x_ssem.at[2 + k], x_rsem.at[2 + k], partner,
            )
        )

    def rows_of(offset):
        return pl.ds(pl.multiple_of(16 * chip(offset), 16), 16)

    for cc in range(2):
        for comp in range(3):
            stage[0, cc, comp, HH] = jnp.zeros((8, F), F32)
    locals_in[0].wait()
    remotes_in[0].wait_recv()
    quarter = pl.multiple_of(8 * xi, 8)
    for i in range(8):
        m = quarter + i
        h, comp = lax.div(m, 3), lax.rem(m, 3)
        ws[m, rows_of(0), :] = jnp.concatenate(
            [stage[0, 0, comp, h], stage[0, 1, comp, h]], axis=0
        ).astype(BF16)

    counts = [8, 8, 8, 3 * HH - 24]

    def span(cnt, dr, last):
        if not last:
            return 0, cnt
        return (0, cnt // 2) if dr == 0 else (cnt // 2, cnt - cnt // 2)

    ag = {}

    def gather_step(unit, step):
        for dr, (peer, sign) in enumerate(dirs):
            if step > 1:
                ag[unit, dr, step - 1].wait_recv()
            if unit == 0:
                ref, base, cnt = ws, quarter, 8
                sems = st_ssem.at[dr, step - 1], st_rsem.at[dr, step - 1]
            else:
                ref, base, cnt = wn, 8 * (unit - 1), counts[unit - 1]
                sems = ag_ssem.at[unit - 1, dr, step - 1], ag_rsem.at[unit - 1, dr, step - 1]
            lo, n = span(cnt, dr, step == far)
            piece = ref.at[pl.ds(base + lo, n), rows_of(-sign * (step - 1)), :]
            ag[unit, dr, step] = remote(piece, piece, sems[0], sems[1], peer)

    gather_step(0, 1)
    locals_in[1].wait()
    remotes_in[1].wait_recv()
    for p in range(PARTS):
        for i in range(counts[p]):
            m = 8 * p + i
            h, comp = m // 3, m % 3
            wn[m, rows_of(0), :] = jnp.concatenate(
                [stage[1, 0, comp, h], stage[1, 1, comp, h]], axis=0
            ).astype(BF16)
        gather_step(1 + p, 1)
    for step in range(2, far + 1):
        for unit in range(1 + PARTS):
            gather_step(unit, step)
        if step == 2:
            swap_tokens(0)
            swap_tokens(1)
        if step == far:
            swap_tokens(2)
            swap_tokens(3)

    sx = {}

    def xgather(i, step):
        for dr, (peer, sign) in enumerate(xdirs):
            lo, n = 4 * i, 4
            if step == 2:
                sx[i, dr, 1].wait_recv()
                lo, n = (4 * i, 2) if dr == 0 else (4 * i + 2, 2)
            base = pl.multiple_of(8 * xpos(-sign * (step - 1)), 8)
            piece = ws.at[pl.ds(base + lo, n)]
            sx[i, dr, step] = remote(
                piece, piece, sx_ssem.at[i, dr, step - 1], sx_rsem.at[i, dr, step - 1], peer
            )

    ag[0, 0, far].wait_recv()
    ag[0, 1, far].wait_recv()
    xgather(0, 1)
    xgather(1, 1)
    pass_word(0)

    def phi(h, xs, ys, w):
        cols = slice(h * D, (h + 1) * D)
        x, y = xs[:, cols], ys[:, cols]
        gu = mm(x, jnp.concatenate([w[3 * h], w[3 * h + 1]], axis=1))
        proj = mm(y, w[3 * h + 2])
        gate, up = gu[:, :F], gu[:, F:]
        s = jax.nn.sigmoid(gate)
        swish = gate * s
        hidden = (swish * up).astype(BF16)
        d_gate = (proj * up * s * (1.0 + gate * (1.0 - s))).astype(BF16)
        d_up = (proj * swish).astype(BF16)
        gab = mm_tn(x, jnp.concatenate([d_gate, d_up], axis=1))
        gc = mm_tn(y, hidden)
        return gate, up, proj, hidden, d_gate, d_up, (gab[:, :F], gab[:, F:], gc)

    def phi_a(h):
        gate, up, proj, hidden, d_gate, d_up, grads = phi(h, xk, xv, ws)
        act[h, 0] = gate
        act[h, 1] = up
        act[h, 2] = proj
        rnd[h, 0] = d_gate
        rnd[h, 1] = d_up
        rnd[h, 2] = hidden
        for i in range(3):
            gbuf[3 * h + i] = grads[i].astype(BF16)

    def phi_b(h):
        grads = phi(h, xq, xo, wn)[-1]
        for i in range(3):
            psum[3 * h + i] = grads[i]
            sbuf[3 * h + i] = grads[i].astype(BF16)

    for pad in (3 * HH, 3 * HH + 1):
        gbuf[pad] = jnp.zeros((D, F), BF16)
        sbuf[pad] = jnp.zeros((D, F), BF16)

    bufs = (gbuf, sbuf)
    rs = {}
    rows_half = D // 2

    def rs_step(k, p, step):
        for dr, (peer, sign) in enumerate(dirs):
            slot = 8 * p + chip(sign * (far + 1 - step))
            lo, n = (0, D)
            if step == 1:
                lo, n = (0, rows_half) if dr == 0 else (rows_half, rows_half)
                src = bufs[k].at[slot, pl.ds(lo, n)]
            else:
                rs[k, p, dr, step - 1].wait_recv()
                if step == 2:
                    a = 0 if dr == 0 else rows_half
                    b = rows_half - a
                    part_sum = bufs[k][slot, a : a + rows_half].astype(F32) + rs_recv[
                        k, p, dr, 0, a : a + rows_half
                    ].astype(F32)
                    rs_send[k, p, dr, 0, a : a + rows_half] = part_sum.astype(BF16)
                    rs_send[k, p, dr, 0, b : b + rows_half] = bufs[k][slot, b : b + rows_half]
                else:
                    total = bufs[k][slot].astype(F32) + rs_recv[k, p, dr, step - 2].astype(F32)
                    rs_send[k, p, dr, step - 2] = total.astype(BF16)
                src = rs_send.at[k, p, dr, step - 2]
            dst = rs_recv.at[k, p, dr, step - 1, pl.ds(lo, n)]
            rs[k, p, dr, step] = remote(
                src, dst, rs_ssem.at[k, p, dr, step - 1], rs_rsem.at[k, p, dr, step - 1], peer
            )

    def rs_total(k, parts):
        out = []
        for p in parts:
            v = bufs[k][8 * p + z].astype(F32)
            for dr in range(2):
                rs[k, p, dr, far].wait_recv()
                v = v + rs_recv[k, p, dr, far - 1].astype(F32)
            out.append(v)
        return out

    groups = ((0, 3), (3, 6), (6, 8), (8, HH))
    for k in range(2):
        locals_in[2 + k].wait()
        remotes_in[2 + k].wait_recv()
    for p in range(PARTS):
        for unit in ((1, 2), (3,), (), (4,))[p]:
            ag[unit, 0, far].wait_recv()
            ag[unit, 1, far].wait_recv()
        for h in range(groups[p][0], groups[p][1]):
            phi_b(h)
        rs_step(1, p, 1)
        if p == 2:
            xgather(0, 2)
    pass_word(1)
    xgather(1, 2)
    for p in range(PARTS):
        rs_step(1, p, 2)
    pass_word(2)
    for p in range(PARTS):
        rs_step(1, p, 3)
    for i in range(2):
        sx[i, 0, 2].wait_recv()
        sx[i, 1, 2].wait_recv()
    for k in range(2):
        locals_in[4 + k].wait()
        remotes_in[4 + k].wait_recv()
    for p in range(PARTS):
        for h in range(groups[p][0], groups[p][1]):
            phi_a(h)
        rs_step(1, p, far)
        rs_step(0, p, 1)
    pass_word(3)
    cts = [(RATE * v).astype(BF16) for v in rs_total(1, range(PARTS))]
    for step in range(2, far + 1):
        for p in range(PARTS):
            rs_step(0, p, step)
    fd = {}

    def field_step(p, step):
        for dr, (peer, sign) in enumerate(dirs):
            if step > 1:
                fd[p, dr, step - 1].wait_recv()
            lo, n = span(D, dr, step == far)
            piece = field.at[8 * p + chip(-sign * (step - 1)), pl.ds(lo, n)]
            fd[p, dr, step] = remote(
                piece, piece, f_ssem.at[p, dr, step - 1], f_rsem.at[p, dr, step - 1], peer
            )

    pass_word(4)
    for pair in ((0, 1), (2, 3)):
        saved = newton_forward(rs_total(0, pair))
        fields = newton_backward(saved, [cts[p] for p in pair])
        for p, value in zip(pair, fields):
            field[8 * p + z] = value.astype(BF16)
            field_step(p, 1)

    def ready(h):
        gate, up, proj = act[h, 0], act[h, 1], act[h, 2]
        s = jax.nn.sigmoid(gate)
        sd = s * (1.0 - s)
        aux[h, 0] = gate * s
        aux[h, 1] = s + gate * sd
        aux[h, 2] = (proj * up) * (sd * (2.0 + gate * (1.0 - 2.0 * s)))

    for step in range(2, far + 1):
        for h in range(HH * (step - 2) // (far - 1), HH * (step - 1) // (far - 1)):
            ready(h)
        for p in range(PARTS):
            field_step(p, step)

    def back(h):
        cols = slice(h * D, (h + 1) * D)
        x, y = xk[:, cols], xv[:, cols]
        up, proj = act[h, 1], act[h, 2]
        swish, q, bend = aux[h, 0], aux[h, 1], aux[h, 2]
        d_gate, d_up, hidden = rnd[h, 0], rnd[h, 1], rnd[h, 2]
        da, db, dc = field[3 * h], field[3 * h + 1], field[3 * h + 2]
        dab = jnp.concatenate([da, db], axis=1)
        ct_gu = mm(x, dab).astype(BF16).astype(F32)
        ct_dg, ct_du = ct_gu[:, :F], ct_gu[:, F:]
        ct_h = mm(y, dc).astype(BF16).astype(F32)
        ct_w = ct_h * up + ct_du * proj
        cq = ct_dg * q
        ct_up = (ct_h * swish + cq * proj).astype(BF16)
        ct_p = (ct_du * swish + cq * up).astype(BF16)
        ct_gate = (ct_w * q + ct_dg * bend).astype(BF16)
        wab = jnp.concatenate([ws[3 * h], ws[3 * h + 1]], axis=1)
        ct_ab = jnp.concatenate([ct_gate, ct_up], axis=1)
        d_ab = jnp.concatenate([d_gate, d_up], axis=1)
        dx = mm_nt(d_ab, dab) + mm_nt(ct_ab, wab)
        dy = mm_nt(hidden, dc) + mm_nt(ct_p, ws[3 * h + 2])
        dk[:, cols] = dx.astype(BF16)
        dv[:, cols] = dy.astype(BF16)
        wg = mm_tn(x, ct_ab)
        tot[3 * h] = (psum[3 * h] + wg[:, :F]).astype(BF16)
        tot[3 * h + 1] = (psum[3 * h + 1] + wg[:, F:]).astype(BF16)
        tot[3 * h + 2] = (psum[3 * h + 2] + mm_tn(y, ct_p)).astype(BF16)

    pass_word(5)

    gr = {}

    def grad_step(p, step):
        cnt = counts[p]
        for dr, (peer, sign) in enumerate(dirs):
            rows = rows_of(sign * (far + 1 - step))
            lo, n = span(cnt, dr, step == 1)
            if step == 1:
                src = tot.at[pl.ds(8 * p + lo, n), rows, :]
            else:
                gr[p, dr, step - 1].wait_recv()
                if step == 2:
                    a, na = span(cnt, dr, True)
                    b, nb = span(cnt, 1 - dr, True)
                    own = tot[8 * p + a : 8 * p + a + na, rows, :].astype(F32)
                    own = own + gr_recv[p, dr, 0, a : a + na].astype(F32)
                    gr_send[p, dr, 0, a : a + na] = own.astype(BF16)
                    gr_send[p, dr, 0, b : b + nb] = tot[8 * p + b : 8 * p + b + nb, rows, :]
                else:
                    own = tot[8 * p : 8 * p + cnt, rows, :].astype(F32)
                    own = own + gr_recv[p, dr, step - 2, :cnt].astype(F32)
                    gr_send[p, dr, step - 2, :cnt] = own.astype(BF16)
                src = gr_send.at[p, dr, step - 2, pl.ds(0, cnt)]
            dst = gr_recv.at[p, dr, step - 1, pl.ds(lo, n)]
            gr[p, dr, step] = remote(
                src, dst, gr_ssem.at[p, dr, step - 1], gr_rsem.at[p, dr, step - 1], peer
            )

    for p in range(PARTS):
        for unit in ((0, 1), (2,), (), (3,))[p]:
            fd[unit, 0, far].wait_recv()
            fd[unit, 1, far].wait_recv()
        for h in range(groups[p][0], groups[p][1]):
            back(h)
        grad_step(p, 1)

    for step in range(2, far + 1):
        for p in range(PARTS):
            grad_step(p, step)
        if step == far - 1:
            outs = []
            for k, (src, dst) in enumerate(((dk, dk_out), (dv, dv_out))):
                cp = remote(
                    src.at[tokens : 2 * tokens], dst.at[:, own_cols], o_ssem.at[k], o_rsem.at[k], partner
                )
                lc = pltpu.make_async_copy(src.at[0:tokens], dst.at[:, own_cols], o_sem.at[k])
                lc.start()
                outs.append((cp, lc))
    send_rows, finish_rows = dp_phase(n_dp, z, c, me, grad_out, *dp_refs)
    for p in range(PARTS):
        cnt = counts[p]
        own = tot[8 * p : 8 * p + cnt, rows_of(0), :].astype(F32)
        for dr in range(2):
            gr[p, dr, far].wait_recv()
            own = own + gr_recv[p, dr, far - 1, :cnt].astype(F32)
        part[0, 8 * p : 8 * p + cnt] = own[:, :8]
        part[1, 8 * p : 8 * p + cnt] = own[:, 8:]
        if cnt < 8:
            part[:, 8 * p + cnt : 8 * p + 8] = jnp.zeros((2, 8 - cnt, 8, F), F32)
        send_rows(p)
    finish_rows()

    for cp in sends:
        cp.wait_send()
    for cp, lc in outs:
        cp.wait_recv()
        lc.wait()


def dp_phase(n, z, c, me, out, part, land, fin, s1, r1, s2, r2):
    per = 32 // n
    other = 1 - c

    def rows_to(j, r):
        return pltpu.make_async_remote_copy(
            src_ref=part.at[r, pl.ds(per * j, per)], dst_ref=land.at[me, c],
            send_sem=s1.at[j, r], recv_sem=r1.at[me, c],
            device_id={"dp": j, "ctx": 2 * z + r}, device_id_type=MESH,
        )

    def rows_from(j, core):
        return pltpu.make_async_remote_copy(
            src_ref=part.at[0, pl.ds(0, per)], dst_ref=land.at[j, core],
            send_sem=s1.at[j, core], recv_sem=r1.at[j, core],
            device_id={"dp": j, "ctx": 2 * z + core}, device_id_type=MESH,
        )

    def spread(k):
        j = lax.rem(me + k, n)
        mine = fin.at[pl.ds(per * me, per)]
        return pltpu.make_async_remote_copy(
            src_ref=mine, dst_ref=mine, send_sem=s2.at[k], recv_sem=r2.at[k],
            device_id={"dp": j}, device_id_type=MESH,
        )

    def send_rows(p):
        for j in range(8 * p // per, 8 * (p + 1) // per):
            for r in range(2):

                @pl.when(2 * me + c != 2 * j + r)
                def _():
                    rows_to(j, r).start()

    def finish_rows():
        rows_from(me, other).wait_recv()
        own = part[c, pl.ds(per * me, per)]
        across = land[me, other]
        first = jnp.where(c == 0, own, across)
        second = jnp.where(c == 0, across, own)

        def take(k, carry):
            j = lax.rem(me + k, n)
            rows_from(j, 0).wait_recv()
            rows_from(j, 1).wait_recv()
            return carry[0] + land[j, 0], carry[1] + land[j, 1]

        first, second = lax.fori_loop(1, n, take, (first, second))
        both = jnp.concatenate([first, second], axis=1) / n
        fin[pl.ds(per * me, per)] = both.astype(BF16)

        def start2(k, carry):
            spread(k).start()
            return carry

        def wait2(k, carry):
            spread(k).wait_recv()
            return carry

        lax.fori_loop(1, n, start2, 0)
        lax.fori_loop(1, n, wait2, 0)
        for h in range(HH):
            for comp in range(3):
                rows = fin[3 * h + comp].astype(F32)
                out[comp, h] = rows[:8]
                out[comp, HH + h] = rows[8:]

        def wait_sent(k, carry):
            j = lax.rem(me + k, n)
            rows_from(j, 0).wait_send()
            rows_from(j, 1).wait_send()
            spread(k).wait_send()
            return carry

        rows_from(me, other).wait_send()
        lax.fori_loop(1, n, wait_sent, 0)

    return send_rows, finish_rows


def land_kernel(dk, dv, gs, dk_out, dv_out, gs_out, b0, b1, b2, in_sems, out_sems):
    trips = ((gs, b2, gs_out), (dk, b0, dk_out), (dv, b1, dv_out))
    loads = [pltpu.make_async_copy(t[0], t[1], in_sems.at[i]) for i, t in enumerate(trips)]
    stores = [pltpu.make_async_copy(t[1], t[2], out_sems.at[i]) for i, t in enumerate(trips)]
    for cp in loads:
        cp.start()
    for load, store in zip(loads, stores):
        load.wait()
        store.start()
    for cp in stores:
        cp.wait()


def dp_scratch(n_dp):
    dma = pltpu.SemaphoreType.DMA
    per = 32 // n_dp
    return [
        pltpu.VMEM((2, 32, 8, F), F32),
        pltpu.VMEM((n_dp, 2, per, 8, F), F32),
        pltpu.VMEM((32, 16, F), BF16),
        dma((n_dp, 2)),
        dma((n_dp, 2)),
        dma((n_dp,)),
        dma((n_dp,)),
    ]


def run(n_dp, n_ctx, keys_a, values_a, queries_b, grad_out, state_start, state_next):
    tokens = keys_a.shape[1]
    nz = n_ctx // 2
    far = nz // 2
    anyspace = pl.BlockSpec(memory_space=pl.ANY)
    vm = pl.BlockSpec(memory_space=pltpu.VMEM)
    flat = (tokens, H * D)
    dma = pltpu.SemaphoreType.DMA
    rows2 = 2 * tokens
    half = HH * D
    token_buf = pltpu.VMEM((rows2, half), BF16)
    mats = pltpu.VMEM((32, D, F), BF16)
    grad_shape = jax.ShapeDtypeStruct((3, H, 8, F), F32)
    dp_list = dp_scratch(n_dp)
    ring_sems = [dma((PARTS, 2, far)), dma((PARTS, 2, far))]
    outs = pl.pallas_call(
        functools.partial(main_kernel, nz, n_dp // NX, n_dp),
        out_shape=(
            jax.ShapeDtypeStruct(flat, BF16),
            jax.ShapeDtypeStruct(flat, BF16),
            grad_shape,
        ),
        in_specs=[pl.BlockSpec(memory_space=pltpu.HBM)] * 6,
        out_specs=(OUT_SPACE, OUT_SPACE, vm),
        scratch_shapes=dp_list
        + [
            token_buf, token_buf, token_buf, token_buf,
            pltpu.VMEM((2, 2, 3, HH + 1, 8, F), F32),
            mats, mats, mats, mats,
            pltpu.VMEM((3 * HH, D, F), F32),
            pltpu.VMEM((2, PARTS, 2, far - 1, D, F), BF16),
            pltpu.VMEM((2, PARTS, 2, far, D, F), BF16),
            mats,
            pltpu.VMEM((HH, 3, rows2, F), F32),
            pltpu.VMEM((HH, 3, rows2, F), F32),
            pltpu.VMEM((HH, 3, rows2, F), BF16),
            token_buf, token_buf,
            mats,
            pltpu.VMEM((PARTS, 2, far - 1, 8, 16, F), BF16),
            pltpu.VMEM((PARTS, 2, far, 8, 16, F), BF16),
            dma((6,)), dma((6,)), dma((6,)),
            dma((2, far)), dma((2, far)),
            dma((2, 2, 2)), dma((2, 2, 2)),
        ]
        + ring_sems
        + [dma((2, PARTS, 2, far)), dma((2, PARTS, 2, far))]
        + ring_sems
        + ring_sems
        + [dma((2,)), dma((2,)), dma((2,)), pltpu.SemaphoreType.REGULAR((NX // 2 + 4,))],
        compiler_params=pltpu.CompilerParams(
            collective_id=0, has_side_effects=True, vmem_limit_bytes=RING_VMEM
        ),
        name="ttt_ring",
    )(
        keys_a.reshape(flat),
        values_a.reshape(flat),
        queries_b.reshape(flat),
        grad_out.reshape(flat),
        state_start,
        state_next[0],
    )
    dk, dv, gs = pl.pallas_call(
        land_kernel,
        out_shape=(
            jax.ShapeDtypeStruct(flat, BF16),
            jax.ShapeDtypeStruct(flat, BF16),
            grad_shape,
        ),
        in_specs=[LAND_SPACE] * 3,
        out_specs=(anyspace,) * 3,
        scratch_shapes=[
            pltpu.VMEM(flat, BF16), pltpu.VMEM(flat, BF16), pltpu.VMEM((3, H, 8, F), F32),
            dma((3,)), dma((3,)),
        ],
        compiler_params=pltpu.CompilerParams(vmem_limit_bytes=LAND_VMEM),
        name="land",
    )(*outs)
    return dk.reshape(keys_a.shape), dv.reshape(keys_a.shape), gs


OUT_SPACE = pl.BlockSpec(memory_space=pl.ANY)
LAND_SPACE = pl.BlockSpec(memory_space=pltpu.HBM)
RING_VMEM = 56 * 1024 * 1024
LAND_VMEM = 56 * 1024 * 1024


def solution(mesh):
    placed = (
        P("dp", "ctx", None),
        P("dp", "ctx", None),
        P("dp", "ctx", None),
        P("dp", "ctx", None),
        P(None, None, "ctx", None),
        P("dp", None, None, "ctx", None),
    )
    return jax.shard_map(
        functools.partial(run, mesh.shape["dp"], mesh.shape["ctx"]),
        mesh=mesh,
        in_specs=placed,
        out_specs=(P("dp", "ctx", None), P("dp", "ctx", None), P(None, None, "ctx", None)),
        check_vma=False,
    )
```
